32 devices in a mesh: tok: 8 (over z, core), voc: 4 (over y, x).
Axes of the slice: x: 2, y: 2, z: 4, core: 2. Of those that a mesh axis runs over, the one named last changes fastest.
Arguments:
- hidden: bfloat16 [4096, 1024], P('tok'), may hold values from -64 to 64
- head_weight: bfloat16 [1024, 16384], P('tok', 'voc'), may hold values from -1 to 1
- target_logits: bfloat16 [4096, 16384], P('tok', 'voc'), may hold values from -320 to 320
- token_ids: int32 [4096], P('tok'), may hold values from 0 to 16383
Outputs:
- loss: float32 [], replicated
- grad_hidden: float32 [4096, 1024], P('tok', 'voc')
- grad_head: float32 [1024, 16384], P('tok', 'voc')
The draws below stay inside these ranges and needn't reach their ends.
All inputs are finite; a program needn't handle non-finite values.
Results may differ from the reference program's by a relative error of at most 0.015.
Values may be sent and summed in bfloat16 or wider, within the bound.
No kernel may reach another device: no remote copies, remote signals or barrier semaphores. Data moves between devices by JAX's collectives and lax.ppermute only.
A program may use at most 128 MiB of HBM per device.

```python
import math
import jax
import jax.numpy as jnp
import numpy as np
from jax import lax

DH = 1024
TOK_DEV = 512
VOCAB = 16384
TOKENS = 4096
N_TOK = 8


def weight_table(key):
    return jax.random.normal(jax.random.fold_in(key, 11), (DH, VOCAB), jnp.float32) / math.sqrt(DH)


def row_rise(top):
    return jnp.exp(jnp.linspace(0.0, math.log(top), TOKENS)).astype(jnp.float32)[:, None]


def draw_head_weight(key, part):
    return jnp.clip(weight_table(key), -1.0, 1.0).astype(jnp.bfloat16)


def draw_hidden(key, part):
    base = 1.5 * row_rise(4.0) * jax.random.normal(jax.random.fold_in(key, 21), (TOKENS, DH), jnp.float32)
    return jnp.clip(base, -64.0, 64.0).astype(jnp.bfloat16)


def draw_target_logits(key, part):
    base = 1.5 * row_rise(4.0) * jax.random.normal(jax.random.fold_in(key, 31), (TOKENS, VOCAB), jnp.float32)
    return jnp.clip(base, -320.0, 320.0).astype(jnp.bfloat16)


def touch_ends(result, key, smallest, top_value):
    spot = [jax.random.randint(jax.random.fold_in(key, axis), (), 0, length) for axis, length in enumerate(result.shape)]
    main_axis = result.shape.index(max(result.shape))
    next_to = spot[:main_axis] + [(spot[main_axis] + 1) % result.shape[main_axis]] + spot[main_axis + 1:]
    return result.at[tuple(spot)].set(smallest).at[tuple(next_to)].set(top_value)


def rank_table(count, skew):
    weights = [(1 << 20) // math.isqrt(grade ** skew) + 1 for grade in range(1, count + 1)]
    spread = 1 + sum(weights) // (1 << 30)
    return np.cumsum(np.array([max(1, weight // spread) for weight in weights]))


def skewed_ids(own_key, dims, number_of, lean):
    table = rank_table(number_of, lean)
    pick = jax.random.randint(jax.random.fold_in(own_key, 1), dims, 0, int(table[number_of - 1]))
    standing = jnp.searchsorted(jnp.asarray(table, jnp.int32), pick, side="right")
    return jax.random.permutation(jax.random.fold_in(own_key, 2), number_of)[standing].astype(jnp.int32)


def setup_inputs(seed: int = 0) -> dict:
    key_list = jax.random.split(jax.random.key(seed), 5)
    return {
        "hidden": draw_hidden(jax.random.fold_in(key_list[4], 71), 0),
        "head_weight": draw_head_weight(jax.random.fold_in(key_list[4], 71), 0),
        "target_logits": draw_target_logits(jax.random.fold_in(key_list[4], 71), 0),
        "token_ids": touch_ends(skewed_ids(key_list[3], (TOKENS,), VOCAB, 2), jax.random.fold_in(key_list[3], 3), 0, VOCAB - 1).astype(jnp.int32),
    }


ce_weight = 0.5


def block_terms(head, hid, target, ids):
    draft = jnp.dot(hid, head, preferred_element_type=jnp.float32)
    target = target.astype(jnp.float32)
    draft_max = jnp.max(draft, axis=1, keepdims=True)
    target_max = jnp.max(target, axis=1, keepdims=True)
    draft_exp = jnp.exp(draft - draft_max)
    target_exp = jnp.exp(target - target_max)
    draft_sum = jnp.sum(draft_exp, axis=1, keepdims=True)
    target_sum = jnp.sum(target_exp, axis=1, keepdims=True)
    probs_q = draft_exp / draft_sum
    probs_p = target_exp / target_sum
    log_q = draft - draft_max - jnp.log(draft_sum)
    log_p = target - target_max - jnp.log(target_sum)
    column = lax.broadcasted_iota(jnp.int32, draft.shape, 1)
    own = (column == ids[:, None].astype(jnp.int32)).astype(jnp.float32)
    kl_part = jnp.sum(probs_p * (log_p - log_q))
    ce_part = -jnp.sum(own * log_q)
    slope = ((1.0 + ce_weight) * probs_q - probs_p - ce_weight * own).astype(jnp.bfloat16)
    grad_hid = jnp.dot(slope, head.T, preferred_element_type=jnp.float32)
    grad_part = jnp.dot(hid.T, slope, preferred_element_type=jnp.float32).astype(jnp.bfloat16).astype(jnp.float32)
    return kl_part + ce_weight * ce_part, grad_hid, grad_part


def reference(hidden, head_weight, target_logits, token_ids):
    hid_blocks = hidden.reshape(N_TOK, TOK_DEV, DH)
    target_blocks = target_logits.reshape(N_TOK, TOK_DEV, VOCAB)
    id_blocks = token_ids.reshape(N_TOK, TOK_DEV)

    def step(carry, xs):
        total, grad_head = carry
        hid, target, ids = xs
        loss_part, grad_hid, grad_part = block_terms(head_weight, hid, target, ids)
        return (total + loss_part, grad_head + grad_part), grad_hid

    start = (jnp.zeros((), jnp.float32), jnp.zeros((DH, VOCAB), jnp.float32))
    (total, grad_head), grad_hidden = lax.scan(step, start, (hid_blocks, target_blocks, id_blocks))
    return total / TOKENS, grad_hidden.reshape(TOKENS, DH), grad_head
```

```python
import functools
import jax
import jax.numpy as jnp
from jax import lax
from jax.sharding import PartitionSpec as P

ce_weight = 0.5
PARTS = 2
f32, bf16 = jnp.float32, jnp.bfloat16


def dot(a, b):
    return lax.dot_general(a, b, (((1,), (0,)), ((), ())), preferred_element_type=f32)


def dot_nt(a, b):
    return lax.dot_general(a, b, (((1,), (1,)), ((), ())), preferred_element_type=f32)


def body(n_tok, n_voc, hidden, head, logits, ids):
    nz = n_tok // 2
    rows, dh = hidden.shape
    share = head.shape[1]
    half = share // 2
    piece = half // PARTS
    deep = 2 * head.shape[0]
    me = lax.axis_index("tok")
    core = lax.rem(me, 2)
    z = lax.div(me, 2)
    voc = lax.axis_index("voc")

    def swap(x):
        return lax.ppermute(x, "tok", [(i, i ^ 1) for i in range(n_tok)])

    def hop(x, pairs):
        return lax.ppermute(x, "tok", [(2 * a + k, 2 * b + k) for a, b in pairs for k in range(2)])

    def cols(x, which, size):
        return lax.dynamic_slice_in_dim(x, which * size, size, 1)

    def combine(fold, x):
        bits = n_voc.bit_length() - 1
        masks = [(k, v) for v in range(min(n_voc, 4)) for k in range(2)]
        rounds = [masks]
        done = 2
        while done < bits:
            wide = min(2, bits - done)
            rounds.append([(0, v << done) for v in range(1 << wide)])
            done += wide
        for masks in rounds:
            got = []
            turned = jnp.concatenate([x[:, rows:], x[:, :rows]], axis=1)
            for k, v in masks:
                if k == 0 and v == 0:
                    got.append(x)
                    continue
                perm = [
                    (t * n_voc + w, (t ^ k) * n_voc + (w ^ v))
                    for t in range(n_tok)
                    for w in range(n_voc)
                ]
                got.append(lax.ppermute(turned if k else x, ("tok", "voc"), perm))
            while len(got) > 1:
                got = [fold(got[j], got[j + 1]) for j in range(0, len(got), 2)]
            x = got[0]
        return x

    def fold_stats(a, b):
        top = jnp.maximum(a[0], b[0])
        total = a[1] * jnp.exp(a[0] - top) + b[1] * jnp.exp(b[0] - top)
        return jnp.concatenate([jnp.stack([top, total]), a[2:] + b[2:]])

    blocks = []
    for p in range(PARTS):
        keep = lax.dynamic_slice_in_dim(head, core * half + p * piece, piece, 1)
        send = lax.dynamic_slice_in_dim(head, (1 - core) * half + p * piece, piece, 1)
        other = swap(send)
        blocks.append(
            jnp.where(
                core == 0,
                jnp.concatenate([keep, other]),
                jnp.concatenate([other, keep]),
            )
        )

    up = [[b] for b in blocks]
    down = [[b] for b in blocks]
    for s in range(1, nz):
        for p in range(PARTS):
            u, d = up[p][-1], down[p][-1]
            up_pairs = [(a, a + 1) for a in range(s - 1, nz - 1)]
            down_pairs = [(a, a - 1) for a in range(1, nz - s + 1)]
            if set(b for _, b in up_pairs) & set(b for _, b in down_pairs) or set(
                a for a, _ in up_pairs
            ) & set(a for a, _ in down_pairs):
                up[p].append(hop(u, up_pairs))
                down[p].append(hop(d, down_pairs))
            else:
                both = hop(jnp.where(z >= s - 1, u, d), up_pairs + down_pairs)
                up[p].append(both)
                down[p].append(both)

    hid = jnp.concatenate([hidden, swap(hidden)])
    hid_t = hid.T
    tgt = jnp.concatenate([cols(logits, core, half), swap(cols(logits, 1 - core, half))])
    tok_ids = jnp.concatenate([ids, swap(ids)])
    target = tgt.astype(f32)
    t_max = jnp.max(target, axis=1)
    t_sum = jnp.sum(jnp.exp(target - t_max[:, None]), axis=1)
    t_top, t_total = combine(fold_stats, jnp.stack([t_max, t_sum]))
    lse_t = t_top + jnp.log(t_total)
    t_inv = 1.0 / t_total
    vocab_start = voc * share + core * half
    iota = lax.broadcasted_iota(jnp.int32, (2 * rows, piece), 1)

    def hid_cols(index):
        return lax.dynamic_slice_in_dim(hid, index * deep, deep, 1)

    draft, whole = [], []
    for p in range(PARTS):
        acc = dot(hid_cols(z), blocks[p])
        for s in range(1, nz):
            u, d = up[p][s], down[p][s]
            if 2 * s < nz:
                acc = acc + dot(hid_cols(jnp.maximum(z - s, 0)), u)
                acc = acc + dot(hid_cols(jnp.minimum(z + s, nz - 1)), d)
            else:
                one = u if u is d else jnp.where(z >= s, u, d)
                index = jnp.where(z >= s, z - s, jnp.minimum(z + s, nz - 1))
                live = jnp.logical_or(z >= s, z + s < nz)
                acc = acc + jnp.where(live, 1.0, 0.0) * dot(hid_cols(index), one)
        draft.append(acc)

    z_max = functools.reduce(jnp.maximum, [jnp.max(a, axis=1) for a in draft])
    z_sum, part_loss = 0.0, 0.0
    probs, owns = [], []
    for p in range(PARTS):
        z_sum = z_sum + jnp.sum(jnp.exp(draft[p] - z_max[:, None]), axis=1)
        t = target[:, p * piece:(p + 1) * piece]
        prob = jnp.exp(t - t_top[:, None]) * t_inv[:, None]
        own = (iota + (vocab_start + p * piece) == tok_ids[:, None]).astype(f32)
        part_loss = part_loss + jnp.sum(
            prob * (t - draft[p]) - ce_weight * own * draft[p], axis=1
        )
        probs.append(prob)
        owns.append(own)
    z_top, z_total, all_loss = combine(fold_stats, jnp.stack([z_max, z_sum, part_loss]))
    lse_z = z_top + jnp.log(z_total)
    scale = (1.0 + ce_weight) * jnp.exp(z_max - z_top) / z_total
    slope = [
        (
            jnp.exp(draft[p] - z_max[:, None]) * scale[:, None]
            - probs[p]
            - ce_weight * owns[p]
        ).astype(bf16)
        for p in range(PARTS)
    ]

    per_token = (all_loss + (1.0 + ce_weight) * lse_z - lse_t).reshape(2, rows)
    plane = jnp.sum(per_token, axis=1)
    plane = jnp.broadcast_to(plane[0] + plane[1], (8, 128))
    spot = lax.broadcasted_iota(jnp.int32, (nz, 1, 1), 0)
    every = jnp.where(spot == z, plane[None], 0.0)
    for k in range(1, nz):
        came = hop(plane, [(a, (a + k) % nz) for a in range(nz)])
        every = every + jnp.where(spot == lax.rem(z - k + nz, nz), came[None], 0.0)
    loss = jnp.sum(every[:, 0, 0]) / (rows * n_tok)

    def grad_rows(index, p):
        return dot(lax.dynamic_slice_in_dim(hid_t, index * deep, deep, 0), slope[p])

    zero = None
    got_up, got_down = [zero] * PARTS, [zero] * PARTS
    for s in range(1, nz):
        for p in range(PARTS):
            up_pairs = [(a, a + 1) for a in range(0, s)]
            down_pairs = [(a, a - 1) for a in range(nz - s, nz)]
            if 2 * s <= nz:
                index = jnp.where(z < s, jnp.minimum(z + nz - s, nz - 1), jnp.maximum(z - nz + s, 0))
                msg = grad_rows(index, p)
                if s > 1:
                    msg = msg + got_up[p].astype(f32)
                    if got_down[p] is not got_up[p]:
                        msg = msg + got_down[p].astype(f32)
                msg = msg.astype(bf16)
                if 2 * s < nz - 1:
                    got_up[p] = got_down[p] = hop(msg, up_pairs + down_pairs)
                else:
                    got_up[p] = hop(msg, up_pairs)
                    got_down[p] = hop(msg, down_pairs)
            else:
                msg_up = grad_rows(jnp.minimum(z + nz - s, nz - 1), p) + got_up[p].astype(f32)
                msg_down = grad_rows(jnp.maximum(z - nz + s, 0), p) + got_down[p].astype(f32)
                got_up[p] = hop(msg_up.astype(bf16), up_pairs)
                got_down[p] = hop(msg_down.astype(bf16), down_pairs)
    keeps, gives = [], []
    for p in range(PARTS):
        full = grad_rows(z, p) + got_up[p].astype(f32) + got_down[p].astype(f32)
        keeps.append(lax.dynamic_slice_in_dim(full, core * (deep // 2), deep // 2, 0))
        give = lax.dynamic_slice_in_dim(full, (1 - core) * (deep // 2), deep // 2, 0)
        gives.append(swap(give.astype(bf16)).astype(f32))
    mine = jnp.concatenate(keeps, axis=1)
    theirs = jnp.concatenate(gives, axis=1)
    grad_head = jnp.where(
        core == 0,
        jnp.concatenate([mine, theirs], axis=1),
        jnp.concatenate([theirs, mine], axis=1),
    )

    part = 0.0
    for p in range(PARTS):
        full = jnp.zeros((dh, piece), bf16)
        for s in range(nz):
            if s == 0:
                block = blocks[p]
            else:
                block = jnp.where(z >= s, up[p][s], down[p][nz - s])
            full = lax.dynamic_update_slice_in_dim(full, block, lax.rem(z - s + nz, nz) * deep, 0)
        part = part + dot_nt(slope[p], full)
    own_part = part[:rows] + swap(part[rows:].astype(bf16)).astype(f32)
    width = dh // n_voc
    grad_hidden = lax.dynamic_slice_in_dim(own_part, voc * width, width, 1)
    for v in range(1, n_voc):
        give = lax.dynamic_slice_in_dim(own_part, (voc ^ v) * width, width, 1).astype(bf16)
        came = lax.ppermute(give, "voc", [(w, w ^ v) for w in range(n_voc)])
        grad_hidden = grad_hidden + came.astype(f32)
    return loss, grad_hidden, grad_head


def solution(mesh):
    placed = (P("tok", None), P("tok", "voc"), P("tok", "voc"), P("tok"))
    return jax.shard_map(
        functools.partial(body, mesh.shape["tok"], mesh.shape["voc"]),
        mesh=mesh,
        in_specs=placed,
        out_specs=(P(), P("tok", "voc"), P("tok", "voc")),
        check_vma=False,
    )
```

```python
import functools
import jax
import jax.numpy as jnp
from jax import lax
from jax.experimental import pallas as pl
from jax.experimental.pallas import tpu as pltpu
from jax.sharding import PartitionSpec as P

ce_weight = 0.5
PARTS = 2
f32, bf16 = jnp.float32, jnp.bfloat16


def dot(a, b):
    return lax.dot_general(a, b, (((1,), (0,)), ((), ())), preferred_element_type=f32)


def dot_nt(a, b):
    return lax.dot_general(a, b, (((1,), (1,)), ((), ())), preferred_element_type=f32)


def lanes(columns, like):
    lane = lax.broadcasted_iota(jnp.int32, like, 1)
    out = jnp.zeros(like, f32)
    for k, c in enumerate(columns):
        out = jnp.where(lane == k, c, out)
    return out


def cost(flops, size, trans=0):
    return pl.CostEstimate(flops=flops, bytes_accessed=size, transcendentals=trans)


PARAMS = pltpu.CompilerParams(vmem_limit_bytes=48 << 20)


def target_kernel(t_ref, e_ref, stat_ref):
    t = t_ref[...].astype(f32)
    top = jnp.max(t, axis=1, keepdims=True)
    e = jnp.exp(t - top)
    e_ref[...] = e.astype(bf16)
    total = jnp.sum(e, axis=1, keepdims=True)
    first = jnp.sum(e * t, axis=1, keepdims=True)
    stat_ref[...] = lanes([top, total, first], stat_ref.shape)


def target_call(tgt, tile):
    n, half = tgt.shape
    return pl.pallas_call(
        target_kernel,
        grid=(n // tile,),
        in_specs=[pl.BlockSpec((tile, half), lambda i: (i, 0))],
        out_specs=[
            pl.BlockSpec((tile, half), lambda i: (i, 0)),
            pl.BlockSpec((tile, 128), lambda i: (i, 0)),
        ],
        out_shape=[
            jax.ShapeDtypeStruct((n, half), bf16),
            jax.ShapeDtypeStruct((n, 128), f32),
        ],
        compiler_params=PARAMS,
        cost_estimate=cost(8 * n * half, 4 * n * half, n * half),
        name="target_exps",
    )(tgt)


def partial_kernel(count, deep, idx_ref, h_ref, *refs):
    out_ref = refs[count]
    acc = None
    for k in range(count):
        at = pl.multiple_of(idx_ref[k] * deep, deep)
        term = dot(h_ref[:, pl.ds(at, deep)], refs[k][...])
        acc = term if acc is None else acc + term
    out_ref[...] = acc


def partial_call(index, hid, terms, tile):
    n, dh = hid.shape
    deep, piece = terms[0].shape
    count = len(terms)
    return pl.pallas_call(
        functools.partial(partial_kernel, count, deep),
        grid_spec=pltpu.PrefetchScalarGridSpec(
            num_scalar_prefetch=1,
            grid=(n // tile,),
            in_specs=[pl.BlockSpec((tile, dh), lambda i, s: (i, 0))]
            + [pl.BlockSpec((deep, piece), lambda i, s: (0, 0))] * count,
            out_specs=pl.BlockSpec((tile, piece), lambda i, s: (i, 0)),
        ),
        out_shape=jax.ShapeDtypeStruct((n, piece), f32),
        compiler_params=PARAMS,
        cost_estimate=cost(2 * n * deep * count * piece, 4 * n * piece + 2 * n * dh),
        name="partial_draft",
    )(index, hid, *terms)


def last_kernel(earlier, idx_ref, h_ref, w_ref, acc_ref, e_ref, id_ref, *refs):
    z = acc_ref[...] + dot(h_ref[...], w_ref[...])
    top = jnp.max(z, axis=1, keepdims=True)
    e = jnp.exp(z - top)
    total = jnp.sum(e, axis=1, keepdims=True)
    cross = jnp.sum(e_ref[...].astype(f32) * z, axis=1, keepdims=True)
    column = lax.broadcasted_iota(jnp.int32, z.shape, 1)
    own = jnp.sum(jnp.where(column == id_ref[...], z, 0.0), axis=1, keepdims=True)
    if earlier is None:
        ez_ref, stat_ref = refs
        ez_ref[...] = e.astype(bf16)
        stat_ref[...] = lanes([top, total, cross, own], stat_ref.shape)
        return
    t_ref = refs[0]
    stat_refs = refs[1:1 + earlier]
    ez_ref, send_ref, turn_ref, tops_ref = refs[1 + earlier:]
    ez_ref[...] = e.astype(bf16)
    tops, all_top = [top], top
    for r in stat_refs:
        tops.insert(len(tops) - 1, r[:, 0:1])
        all_top = jnp.maximum(all_top, r[:, 0:1])
    total = total * jnp.exp(top - all_top)
    for r in stat_refs:
        total = total + r[:, 1:2] * jnp.exp(r[:, 0:1] - all_top)
        cross = cross + r[:, 2:3]
        own = own + r[:, 3:4]
    t_top, t_total, t_first = t_ref[:, 0:1], t_ref[:, 1:2], t_ref[:, 2:3]
    like = t_ref.shape
    rows = lanes([t_top, t_total, t_first - cross, all_top, total, own], like).T[:8]
    send_ref[...] = rows
    turn_ref[...] = rows
    tops_ref[...] = lanes([t_top] + tops, like)


def last_call(index, hid, w, acc, e_t, part, ids, t_stat, stats, tile):
    n, dh = hid.shape
    deep, piece = w.shape
    grid = n // tile
    row = lambda i, s: (i, 0)
    in_specs = [
        pl.BlockSpec((tile, deep), lambda i, s: (i, s[0])),
        pl.BlockSpec((deep, piece), lambda i, s: (0, 0)),
        pl.BlockSpec((tile, piece), row),
        pl.BlockSpec((tile, piece), lambda i, s: (i, part)),
        pl.BlockSpec((tile, 1), row),
    ]
    args = [hid, w, acc, e_t, ids]
    out_specs = [pl.BlockSpec((tile, piece), row)]
    out_shape = [jax.ShapeDtypeStruct((n, piece), bf16)]
    earlier = None
    if stats is None:
        out_specs += [pl.BlockSpec((tile, 128), row)]
        out_shape += [jax.ShapeDtypeStruct((n, 128), f32)]
    else:
        earlier = len(stats)
        args += [t_stat] + stats
        in_specs += [pl.BlockSpec((tile, 128), row)] * (1 + earlier)
        out_specs += [
            pl.BlockSpec((8, tile), lambda i, s: (0, i)),
            pl.BlockSpec((8, tile), lambda i, s: (0, lax.rem(i + grid // 2, grid))),
            pl.BlockSpec((tile, 128), row),
        ]
        out_shape += [
            jax.ShapeDtypeStruct((8, n), f32),
            jax.ShapeDtypeStruct((8, n), f32),
            jax.ShapeDtypeStruct((n, 128), f32),
        ]
    return pl.pallas_call(
        functools.partial(last_kernel, earlier),
        grid_spec=pltpu.PrefetchScalarGridSpec(
            num_scalar_prefetch=1, grid=(grid,), in_specs=in_specs, out_specs=out_specs
        ),
        out_shape=out_shape,
        compiler_params=PARAMS,
        cost_estimate=cost(2 * n * deep * piece, 8 * n * piece, n * piece),
        name="last_draft",
    )(index, *args)


def fold_rows(a, b):
    t_top = jnp.maximum(a[0:1], b[0:1])
    fa, fb = jnp.exp(a[0:1] - t_top), jnp.exp(b[0:1] - t_top)
    z_top = jnp.maximum(a[3:4], b[3:4])
    ga, gb = jnp.exp(a[3:4] - z_top), jnp.exp(b[3:4] - z_top)
    rows = [
        t_top,
        a[1:2] * fa + b[1:2] * fb,
        a[2:3] * fa + b[2:3] * fb,
        z_top,
        a[4:5] * ga + b[4:5] * gb,
        a[5:6] + b[5:6],
    ]
    return jnp.concatenate(rows + [a[6:8]])


def slope_kernel(part, peers, idx_ref, *refs):
    step = pl.program_id(0)
    if peers:
        tops_ref = refs[peers]
        ez_ref, et_ref, id_ref, ht_ref = refs[peers + 1:peers + 5]
        slope_ref, msg_ref, coef_ref, loss_ref = refs[peers + 5:]

        @pl.when(step == 0)
        def _():
            got = [r[...] for r in refs[:peers]]
            while len(got) > 1:
                got = [fold_rows(got[j], got[j + 1]) for j in range(0, len(got), 2)]
            s = got[0]
            t_inv = 1.0 / s[1:2]
            lse_t = s[0:1] + jnp.log(s[1:2])
            lse_z = s[3:4] + jnp.log(s[4:5])
            n = s.shape[1]
            per_token = s[2:3] * t_inv - lse_t + (1.0 + ce_weight) * lse_z - ce_weight * s[5:6]
            plane = jnp.sum(per_token[:, :n // 2], axis=1, keepdims=True) + jnp.sum(
                per_token[:, n // 2:], axis=1, keepdims=True
            )
            loss_ref[...] = jnp.broadcast_to(plane, loss_ref.shape)
            z_inv = (1.0 + ce_weight) / s[4:5]
            flat = jnp.concatenate([s[0:1], t_inv, s[3:4], z_inv, jnp.zeros((124, n), f32)]).T
            tops = tops_ref[...]
            lane = lax.broadcasted_iota(jnp.int32, tops.shape, 1)
            base = jnp.where(lane == 0, flat[:, 0:1], flat[:, 2:3])
            gain = jnp.where(lane == 0, flat[:, 1:2], flat[:, 3:4])
            coef_ref[...] = jnp.where(lane <= PARTS, jnp.exp(tops - base) * gain, 0.0)

    else:
        coef_ref, ez_ref, et_ref, id_ref, ht_ref, slope_ref, msg_ref = refs
    b = coef_ref[:, 0:1]
    a = coef_ref[:, part + 1:part + 2]
    value = ez_ref[...].astype(f32) * a - et_ref[...].astype(f32) * b
    column = lax.broadcasted_iota(jnp.int32, value.shape, 1) + step * value.shape[1]
    value = jnp.where(column == id_ref[...], value - ce_weight, value)
    slope = value.astype(bf16)
    slope_ref[...] = slope
    msg_ref[...] = dot(ht_ref[...], slope).astype(bf16)


def slope_call(part, index, head_args, e_z, e_t, ids, hid_t, deep, tile):
    n, piece = e_z.shape
    peers = len(head_args) - 1
    steps = piece // tile
    fixed = lambda i, s: (0, 0)
    in_specs = [pl.BlockSpec(a.shape, fixed) for a in head_args] + [
        pl.BlockSpec((n, tile), lambda i, s: (0, i)),
        pl.BlockSpec((n, tile), lambda i, s: (0, part * steps + i)),
        pl.BlockSpec((n, 1), fixed),
        pl.BlockSpec((deep, n), lambda i, s: (s[0], 0)),
    ]
    out_specs = [
        pl.BlockSpec((n, tile), lambda i, s: (0, i)),
        pl.BlockSpec((deep, tile), lambda i, s: (0, i)),
    ]
    out_shape = [
        jax.ShapeDtypeStruct((n, piece), bf16),
        jax.ShapeDtypeStruct((deep, piece), bf16),
    ]
    if peers:
        out_specs += [pl.BlockSpec((n, 128), fixed), pl.BlockSpec((8, 128), fixed)]
        out_shape += [
            jax.ShapeDtypeStruct((n, 128), f32),
            jax.ShapeDtypeStruct((8, 128), f32),
        ]
    return pl.pallas_call(
        functools.partial(slope_kernel, part, peers),
        grid_spec=pltpu.PrefetchScalarGridSpec(
            num_scalar_prefetch=1, grid=(steps,), in_specs=in_specs, out_specs=out_specs
        ),
        out_shape=out_shape,
        compiler_params=PARAMS,
        cost_estimate=cost(2 * n * deep * piece, 6 * n * piece),
        name="slope",
    )(index, *head_args, e_z, e_t, ids, hid_t)


def body(n_tok, n_voc, hidden, head, logits, ids):
    nz = n_tok // 2
    rows, dh = hidden.shape
    own_rows, share = head.shape
    half = share // 2
    piece = half // PARTS
    deep = 2 * own_rows
    tile = min(256, rows)
    me = lax.axis_index("tok")
    core = lax.rem(me, 2)
    z = lax.div(me, 2)
    voc = lax.axis_index("voc")

    def swap(x):
        return lax.ppermute(x, "tok", [(i, i ^ 1) for i in range(n_tok)])

    def hop(x, pairs):
        return lax.ppermute(x, "tok", [(2 * a + k, 2 * b + k) for a, b in pairs for k in range(2)])

    def plane_swap(x, v):
        return lax.ppermute(x, "voc", [(w, w ^ v) for w in range(n_voc)])

    def mine(x, other=False):
        left, right = x[:, :half], x[:, half:]
        return jnp.where((core == 0) != other, left, right)

    def flip(x):
        parts = [x[:, (k ^ 1) * own_rows:((k ^ 1) + 1) * own_rows] for k in range(2 * nz)]
        return jnp.where(core == 0, x, jnp.concatenate(parts, axis=1))

    def scalar(x):
        return jnp.reshape(x, (1,)).astype(jnp.int32)

    keep, send = mine(head), mine(head, True)
    blocks = []
    for p in range(PARTS):
        cut = slice(p * piece, (p + 1) * piece)
        blocks.append(jnp.concatenate([keep[:, cut], swap(send[:, cut])]))

    up = [[b] for b in blocks]
    down = [[b] for b in blocks]
    merged = [None] * nz
    for s in range(1, nz):
        up_pairs = [(a, a + 1) for a in range(s - 1, nz - 1)]
        down_pairs = [(a, a - 1) for a in range(1, nz - s + 1)]
        for p in range(PARTS):
            u, d = up[p][-1], down[p][-1]
            if 2 * s > nz + 1:
                both = hop(jnp.where(z >= s - 1, u, d), up_pairs + down_pairs)
                up[p].append(both)
                down[p].append(both)
            else:
                up[p].append(hop(u, up_pairs))
                down[p].append(hop(d, down_pairs))

    def arrived(p, s):
        u, d = up[p][s], down[p][s]
        if u is d:
            return [(jnp.where(z >= s, nz - s, s), u)]
        if 2 * s >= nz:
            return [(jnp.where(z >= s, nz - s, s), jnp.where(z >= s, u, d))]
        return [(nz - s, u), (s, d)]

    hid = flip(jnp.concatenate([hidden, swap(hidden)]))
    hid = lax.dynamic_slice_in_dim(jnp.concatenate([hid, hid], axis=1), z * deep, dh, 1)
    hid_t = hid.T
    tgt = jnp.concatenate([mine(logits), swap(mine(logits, True))])
    local = jnp.concatenate([ids, swap(ids)]) - (voc * share + core * half)
    local = [(local - p * piece)[:, None] for p in range(PARTS)]
    e_t, t_stat = target_call(tgt, tile)

    stats, e_z = [], []
    for p in range(PARTS):
        terms = [(0, blocks[p])] + [x for s in range(1, nz - 1) for x in arrived(p, s)]
        index = jnp.stack([jnp.asarray(k, jnp.int32) for k, _ in terms])
        acc = partial_call(index, hid, [w for _, w in terms], tile)
        final = arrived(p, nz - 1)
        assert len(final) == 1
        at, w = final[0]
        at = scalar(jnp.minimum(at, nz - 1))
        if p < PARTS - 1:
            e, st = last_call(at, hid, w, acc, e_t, p, local[p], None, None, tile)
            stats.append(st)
        else:
            e, mine_rows, turned, tops = last_call(
                at, hid, w, acc, e_t, p, local[p], t_stat, stats, tile
            )
        e_z.append(e)

    x = fold_rows(mine_rows, swap(turned))
    bits = n_voc.bit_length() - 1
    done = 0
    while True:
        wide = min(2, bits - done)
        got = [x] + [plane_swap(x, v << done) for v in range(1, 1 << wide)]
        done += wide
        if done >= bits:
            break
        while len(got) > 1:
            got = [fold_rows(got[j], got[j + 1]) for j in range(0, len(got), 2)]
        x = got[0]

    def first_row(s):
        return jnp.where(z < s, nz - s, s)

    msgs, slope = [], []
    for p in range(PARTS):
        head_args = got + [tops] if p == 0 else [coef]
        outs = slope_call(
            p, scalar(first_row(1)), head_args, e_z[p], e_t, local[p], hid_t, deep, tile
        )
        slope.append(outs[0])
        msgs.append(outs[1])
        if p == 0:
            coef, plane = outs[2:]

    def grad_rows(index, p):
        return dot(lax.dynamic_slice_in_dim(hid_t, index * deep, deep, 0), slope[p])

    got_up, got_down = [None] * PARTS, [None] * PARTS
    for s in range(1, nz):
        up_pairs = [(a, a + 1) for a in range(0, s)]
        down_pairs = [(a, a - 1) for a in range(nz - s, nz)]
        for p in range(PARTS):
            if 2 * s <= nz:
                if s == 1:
                    msg = msgs[p]
                else:
                    msg = grad_rows(first_row(s), p) + got_up[p].astype(f32)
                    if got_down[p] is not got_up[p]:
                        msg = msg + got_down[p].astype(f32)
                    msg = msg.astype(bf16)
                if 2 * s < nz - 1:
                    got_up[p] = got_down[p] = hop(msg, up_pairs + down_pairs)
                else:
                    got_up[p] = hop(msg, up_pairs)
                    got_down[p] = hop(msg, down_pairs)
            else:
                msg_up = grad_rows(nz - s, p) + got_up[p].astype(f32)
                msg_down = grad_rows(s, p) + got_down[p].astype(f32)
                got_up[p] = hop(msg_up.astype(bf16), up_pairs)
                got_down[p] = hop(msg_down.astype(bf16), down_pairs)
    keeps, gives = [], []
    for p in range(PARTS):
        full = grad_rows(0, p) + got_up[p].astype(f32) + got_down[p].astype(f32)
        keeps.append(full[:own_rows])
        gives.append(swap(full[own_rows:].astype(bf16)).astype(f32))
    grad_head = jnp.where(
        core == 0,
        jnp.concatenate(keeps + gives, axis=1),
        jnp.concatenate(gives + keeps, axis=1),
    )

    late, plane, _ = lax.optimization_barrier((slope, plane, msgs[-1]))
    spot = lax.broadcasted_iota(jnp.int32, (nz, 1, 1), 0)
    every = jnp.where(spot == z, plane[None], 0.0)
    for k in range(1, nz):
        came = hop(plane, [(a, (a + k) % nz) for a in range(nz)])
        every = every + jnp.where(spot == lax.rem(z - k + nz, nz), came[None], 0.0)
    loss = jnp.sum(every[:, 0, 0]) / (rows * n_tok)

    part = 0.0
    for p in range(PARTS):
        ring = [blocks[p]]
        for j in range(1, nz):
            ring.append(jnp.where(z + j < nz, down[p][j], up[p][nz - j]))
        part = part + dot_nt(late[p], jnp.concatenate(ring))
    own_part = flip(part[:rows]) + swap(flip(part[rows:].astype(bf16))).astype(f32)
    twice = jnp.concatenate([own_part, own_part], axis=1)
    width = dh // n_voc

    def wide_slice(w):
        return lax.dynamic_slice_in_dim(twice, lax.rem(w * width - z * deep + dh, dh), width, 1)

    grad_hidden = wide_slice(voc)
    for v in range(1, n_voc):
        give = wide_slice(voc ^ v).astype(bf16)
        grad_hidden = grad_hidden + plane_swap(give, v).astype(f32)
    return loss, grad_hidden, grad_head


def solution(mesh):
    placed = (P("tok", None), P("tok", "voc"), P("tok", "voc"), P("tok"))
    return jax.shard_map(
        functools.partial(body, mesh.shape["tok"], mesh.shape["voc"]),
        mesh=mesh,
        in_specs=placed,
        out_specs=(P(), P("tok", "voc"), P("tok", "voc")),
        check_vma=False,
    )
```

```python
import functools
import jax
import jax.numpy as jnp
from jax import lax
from jax.experimental import pallas as pl
from jax.experimental.pallas import tpu as pltpu
from jax.sharding import PartitionSpec as P


ce_weight = 0.5
PARTS = 2
f32, bf16 = jnp.float32, jnp.bfloat16


def dot(a, b):
    return lax.dot_general(a, b, (((1,), (0,)), ((), ())), preferred_element_type=f32)


def dot_nt(a, b):
    return lax.dot_general(a, b, (((1,), (1,)), ((), ())), preferred_element_type=f32)


def lanes(columns, like):
    lane = lax.broadcasted_iota(jnp.int32, like, 1)
    out = jnp.zeros(like, f32)
    for k, c in enumerate(columns):
        out = jnp.where(lane == k, c, out)
    return out


def cost(flops, size, trans=0):
    return pl.CostEstimate(flops=flops, bytes_accessed=size, transcendentals=trans)


def hbm(x):
    return pltpu.with_memory_space_constraint(x, pltpu.HBM)


def out(shape, dtype):
    return pltpu.HBM(shape, dtype)


def params(size):
    return pltpu.CompilerParams(vmem_limit_bytes=size << 20)


def target_kernel(own_tiles, core_ref, mine_ref, came_ref, id_ref, e_ref, stat_ref):
    t = jnp.where(pl.program_id(0) < own_tiles, mine_ref[...], came_ref[...]).astype(f32)
    top = jnp.max(t, axis=1, keepdims=True)
    e = jnp.exp(t - top)
    e_ref[...] = e.astype(bf16)
    total = jnp.sum(e, axis=1, keepdims=True)
    first = jnp.sum(e * t, axis=1, keepdims=True)
    stat_ref[...] = lanes([top, total, first, id_ref[...].astype(f32)], stat_ref.shape)


def target_call(core, logits, came, ids, tile):
    rows, half = came.shape
    n, own_tiles = 2 * rows, rows // tile
    row = lambda i, s: (i, 0)
    return pl.pallas_call(
        functools.partial(target_kernel, own_tiles),
        grid_spec=pltpu.PrefetchScalarGridSpec(
            num_scalar_prefetch=1,
            grid=(n // tile,),
            in_specs=[
                pl.BlockSpec((tile, half), lambda i, s: (jnp.minimum(i, own_tiles - 1), s[0])),
                pl.BlockSpec((tile, half), lambda i, s: (jnp.maximum(i - own_tiles, 0), 0)),
                pl.BlockSpec((tile, 1), row),
            ],
            out_specs=[pl.BlockSpec((tile, half), row), pl.BlockSpec((tile, 128), row)],
        ),
        out_shape=[
            out((n, half), bf16),
            jax.ShapeDtypeStruct((n, 128), f32),
        ],
        compiler_params=params(20),
        cost_estimate=cost(8 * n * half, 4 * n * half, n * half),
        name="target_exps",
    )(core, hbm(logits), hbm(came), ids)


def turn_kernel(x_ref, out_ref):
    out_ref[...] = x_ref[...].T


def turn_call(x, tile):
    n, dh = x.shape
    return pl.pallas_call(
        turn_kernel,
        grid=(n // tile,),
        in_specs=[pl.BlockSpec((tile, dh), lambda i: (i, 0))],
        out_specs=pl.BlockSpec((dh, tile), lambda i: (0, i)),
        out_shape=out((dh, n), bf16),
        compiler_params=params(16),
        cost_estimate=cost(0, 4 * n * dh),
        name="turn",
    )(x)


def choices(nz):
    unique, table = [("own", 0)], []
    for j in range(1, nz):
        table.append((("down", j), ("up", nz - j)))
        unique += [c for c in table[-1] if c not in unique]
    return unique, table


def gathered(up, down, p, nz):
    unique, _ = choices(nz)
    pick = {"own": up, "up": up, "down": down}
    return [pick[k][p][j] for k, j in unique]


def assemble(z, nz, refs, whole_ref, sem):
    unique, table = choices(nz)
    deep = refs[0].shape[0]

    def copy(k, j):
        at = pl.multiple_of(lax.rem(z + j, nz) * deep, deep)
        return pltpu.make_async_copy(refs[k], whole_ref.at[pl.ds(at, deep), :], sem.at[j])

    copy(0, 0).start()
    for j in range(1, nz):
        near, far = (unique.index(c) for c in table[j - 1])

        @pl.when(z + j < nz)
        def _(near=near, j=j):
            copy(near, j).start()

        @pl.when(z + j >= nz)
        def _(far=far, j=j):
            copy(far, j).start()

    return lambda: [copy(0, j).wait() for j in range(nz)]


def last_kernel(part, nz, count, earlier, z_ref, *refs):
    w_refs, refs = refs[:count], refs[count:]
    h_ref, e_ref, t_ref = refs[:3]
    stat_refs = refs[3:3 + earlier]
    outs = refs[3 + earlier:-2]
    whole_ref, sem = refs[-2:]

    @pl.when(pl.program_id(0) == 0)
    def _():
        assemble(z_ref[0], nz, w_refs, whole_ref, sem)()

    z = dot(h_ref[...], whole_ref[...])
    top = jnp.max(z, axis=1, keepdims=True)
    e = jnp.exp(z - top)
    outs[0][...] = e.astype(bf16)
    total = jnp.sum(e, axis=1, keepdims=True)
    cross = jnp.sum(e_ref[...].astype(f32) * z, axis=1, keepdims=True)
    t_stat = t_ref[...]
    column = lax.broadcasted_iota(jnp.int32, z.shape, 1) + part * z.shape[1]
    id_col = t_stat[:, 3:4].astype(jnp.int32)
    own = jnp.sum(jnp.where(column == id_col, z, 0.0), axis=1, keepdims=True)
    like = t_ref.shape
    if part < PARTS - 1:
        outs[1][...] = lanes([top, total, cross, own], like)
        return
    send_ref, turn_ref, tops_ref = outs[1:]
    tops, all_top = [], top
    for r in stat_refs:
        tops.append(r[:, 0:1])
        all_top = jnp.maximum(all_top, r[:, 0:1])
    tops.append(top)
    total = total * jnp.exp(top - all_top)
    for r in stat_refs:
        total = total + r[:, 1:2] * jnp.exp(r[:, 0:1] - all_top)
        cross = cross + r[:, 2:3]
        own = own + r[:, 3:4]
    t_top, t_total, t_first = t_stat[:, 0:1], t_stat[:, 1:2], t_stat[:, 2:3]
    rows = lanes([t_top, t_total, t_first - cross, all_top, total, own], like).T[:8]
    send_ref[...] = rows
    turn_ref[...] = rows
    tops_ref[...] = lanes([t_top] + tops + [t_stat[:, 3:4]], like)


def last_call(part, nz, z, blocks, hid, e_t, t_stat, stats, tile):
    n, dh = hid.shape
    piece = blocks[0].shape[1]
    grid = n // tile
    row = lambda i, s: (i, 0)
    stat_spec = pl.BlockSpec((tile, 128), row)
    in_specs = [pl.BlockSpec(memory_space=pl.ANY)] * len(blocks) + [
        pl.BlockSpec((tile, dh), row),
        pl.BlockSpec((tile, piece), lambda i, s: (i, part)),
        stat_spec,
    ]
    out_specs = [pl.BlockSpec((tile, piece), row)]
    out_shape = [out((n, piece), bf16)]
    if part < PARTS - 1:
        stats = []
        out_specs += [stat_spec]
        out_shape += [jax.ShapeDtypeStruct((n, 128), f32)]
    else:
        in_specs += [stat_spec] * len(stats)
        out_specs += [
            pl.BlockSpec((8, tile), lambda i, s: (0, i)),
            pl.BlockSpec((8, tile), lambda i, s: (0, lax.rem(i + grid // 2, grid))),
            stat_spec,
        ]
        out_shape += [
            jax.ShapeDtypeStruct((8, n), f32),
            jax.ShapeDtypeStruct((8, n), f32),
            jax.ShapeDtypeStruct((n, 128), f32),
        ]
    return pl.pallas_call(
        functools.partial(last_kernel, part, nz, len(blocks), len(stats)),
        grid_spec=pltpu.PrefetchScalarGridSpec(
            num_scalar_prefetch=1,
            grid=(grid,),
            in_specs=in_specs,
            out_specs=out_specs,
            scratch_shapes=[pltpu.VMEM((dh, piece), bf16), pltpu.SemaphoreType.DMA((nz,))],
        ),
        out_shape=out_shape,
        compiler_params=params(20),
        cost_estimate=cost(2 * n * dh * piece, 6 * n * piece, n * piece),
        name="last_draft",
    )(z, *blocks, hbm(hid), hbm(e_t), t_stat, *stats)


def hidden_kernel(nz, count, z_ref, *refs):
    slope_refs, w_refs = refs[:PARTS], refs[PARTS:PARTS + PARTS * count]
    out_ref, whole_ref, sem = refs[PARTS + PARTS * count:]

    @pl.when(pl.program_id(0) == 0)
    def _():
        waits = [
            assemble(z_ref[0], nz, w_refs[p * count:(p + 1) * count], whole_ref.at[p], sem.at[p])
            for p in range(PARTS)
        ]
        for wait in waits:
            wait()

    acc = dot_nt(slope_refs[0][...], whole_ref[0])
    for p in range(1, PARTS):
        acc = acc + dot_nt(slope_refs[p][...], whole_ref[p])
    out_ref[...] = acc.astype(bf16)


def hidden_call(nz, z, slope, blocks, dh, tile):
    n, piece = slope[0].shape
    count = len(blocks[0])
    row = lambda i, s: (i, 0)
    return pl.pallas_call(
        functools.partial(hidden_kernel, nz, count),
        grid_spec=pltpu.PrefetchScalarGridSpec(
            num_scalar_prefetch=1,
            grid=(n // tile,),
            in_specs=[pl.BlockSpec((tile, piece), row)] * PARTS
            + [pl.BlockSpec(memory_space=pl.ANY)] * (PARTS * count),
            out_specs=pl.BlockSpec((tile, dh), row),
            scratch_shapes=[
                pltpu.VMEM((PARTS, dh, piece), bf16),
                pltpu.SemaphoreType.DMA((PARTS, nz)),
            ],
        ),
        out_shape=out((n, dh), bf16),
        compiler_params=params(20),
        cost_estimate=cost(2 * n * dh * piece * PARTS, 8 * n * piece),
        name="hidden_grad",
    )(z, *map(hbm, slope), *[b for bs in blocks for b in bs])


def fold_rows(a, b):
    t_top = jnp.maximum(a[0:1], b[0:1])
    fa, fb = jnp.exp(a[0:1] - t_top), jnp.exp(b[0:1] - t_top)
    z_top = jnp.maximum(a[3:4], b[3:4])
    ga, gb = jnp.exp(a[3:4] - z_top), jnp.exp(b[3:4] - z_top)
    rows = [
        t_top,
        a[1:2] * fa + b[1:2] * fb,
        a[2:3] * fa + b[2:3] * fb,
        z_top,
        a[4:5] * ga + b[4:5] * gb,
        a[5:6] + b[5:6],
    ]
    return jnp.concatenate(rows + [a[6:8]])


def slope_kernel(part, peers, idx_ref, *refs):
    step = pl.program_id(0)
    if peers:
        tops_ref = refs[peers]
        ez_ref, et_ref, ht_ref = refs[peers + 1:peers + 4]
        slope_ref, msg_ref, coef_ref, loss_ref = refs[peers + 4:]

        @pl.when(step == 0)
        def _():
            got = [r[...] for r in refs[:peers]]
            while len(got) > 1:
                got = [fold_rows(got[j], got[j + 1]) for j in range(0, len(got), 2)]
            s = got[0]
            t_inv = 1.0 / s[1:2]
            lse_t = s[0:1] + jnp.log(s[1:2])
            lse_z = s[3:4] + jnp.log(s[4:5])
            n = s.shape[1]
            per_token = s[2:3] * t_inv - lse_t + (1.0 + ce_weight) * lse_z - ce_weight * s[5:6]
            plane = jnp.sum(per_token[:, :n // 2], axis=1, keepdims=True) + jnp.sum(
                per_token[:, n // 2:], axis=1, keepdims=True
            )
            loss_ref[...] = jnp.broadcast_to(plane, loss_ref.shape)
            z_inv = (1.0 + ce_weight) / s[4:5]
            flat = jnp.concatenate([s[0:1], t_inv, s[3:4], z_inv, jnp.zeros((124, n), f32)]).T
            tops = tops_ref[...]
            lane = lax.broadcasted_iota(jnp.int32, tops.shape, 1)
            base = jnp.where(lane == 0, flat[:, 0:1], flat[:, 2:3])
            gain = jnp.where(lane == 0, flat[:, 1:2], flat[:, 3:4])
            coef_ref[...] = jnp.where(lane <= PARTS, jnp.exp(tops - base) * gain, tops)

    else:
        coef_ref, ez_ref, et_ref, ht_ref, slope_ref, msg_ref = refs
    b = coef_ref[:, 0:1]
    a = coef_ref[:, part + 1:part + 2]
    value = ez_ref[...].astype(f32) * a - et_ref[...].astype(f32) * b
    column = lax.broadcasted_iota(jnp.int32, value.shape, 1)
    tile = value.shape[1]
    start = (part * pl.num_programs(0) + step) * tile
    id_col = coef_ref[:, PARTS + 1:PARTS + 2].astype(jnp.int32) - start
    value = jnp.where(column == id_col, value - ce_weight, value)
    slope = value.astype(bf16)
    slope_ref[...] = slope
    msg_ref[...] = dot(ht_ref[...], slope).astype(bf16)


def slope_call(part, index, head_args, e_z, e_t, hid_t, deep, tile):
    n, piece = e_z.shape
    peers = len(head_args) - 1
    steps = piece // tile
    fixed = lambda i, s: (0, 0)
    in_specs = [pl.BlockSpec(a.shape, fixed) for a in head_args] + [
        pl.BlockSpec((n, tile), lambda i, s: (0, i)),
        pl.BlockSpec((n, tile), lambda i, s: (0, part * steps + i)),
        pl.BlockSpec((deep, n), lambda i, s: (s[0], 0)),
    ]
    out_specs = [
        pl.BlockSpec((n, tile), lambda i, s: (0, i)),
        pl.BlockSpec((deep, tile), lambda i, s: (0, i)),
    ]
    out_shape = [
        out((n, piece), bf16),
        out((deep, piece), bf16),
    ]
    if peers:
        out_specs += [pl.BlockSpec((n, 128), fixed), pl.BlockSpec((8, 128), fixed)]
        out_shape += [
            jax.ShapeDtypeStruct((n, 128), f32),
            jax.ShapeDtypeStruct((8, 128), f32),
        ]
    return pl.pallas_call(
        functools.partial(slope_kernel, part, peers),
        grid_spec=pltpu.PrefetchScalarGridSpec(
            num_scalar_prefetch=1, grid=(steps,), in_specs=in_specs, out_specs=out_specs
        ),
        out_shape=out_shape,
        compiler_params=params(28),
        cost_estimate=cost(2 * n * deep * piece, 6 * n * piece),
        name="slope",
    )(index, *head_args, hbm(e_z), hbm(e_t), hbm(hid_t))


def body(n_tok, n_voc, hidden, head, logits, ids):
    nz = n_tok // 2
    rows, dh = hidden.shape
    own_rows, share = head.shape
    half = share // 2
    piece = half // PARTS
    deep = 2 * own_rows
    tile = min(256, rows)
    wide = min(512, piece)
    me = lax.axis_index("tok")
    core = lax.rem(me, 2)
    z = lax.div(me, 2)
    voc = lax.axis_index("voc")

    def swap(x):
        return lax.ppermute(x, "tok", [(i, i ^ 1) for i in range(n_tok)])

    def hop(x, pairs):
        return lax.ppermute(x, "tok", [(2 * a + k, 2 * b + k) for a, b in pairs for k in range(2)])

    def plane_swap(x, v):
        return lax.ppermute(x, "voc", [(w, w ^ v) for w in range(n_voc)])

    def mine(x, other=False):
        return jnp.where((core == 0) != other, x[:, :half], x[:, half:])

    def scalar(x):
        return jnp.reshape(x, (1,)).astype(jnp.int32)

    keep, send = mine(head), mine(head, True)
    blocks = []
    for p in range(PARTS):
        cut = slice(p * piece, (p + 1) * piece)
        other = swap(send[:, cut])
        blocks.append(
            jnp.where(
                core == 0,
                jnp.concatenate([keep[:, cut], other]),
                jnp.concatenate([other, keep[:, cut]]),
            )
        )

    up = [[b] for b in blocks]
    down = [[b] for b in blocks]
    for s in range(1, nz):
        up_pairs = [(a, a + 1) for a in range(s - 1, nz - 1)]
        down_pairs = [(a, a - 1) for a in range(1, nz - s + 1)]
        for p in range(PARTS):
            u, d = up[p][-1], down[p][-1]
            if 2 * s > nz + 1:
                both = hop(jnp.where(z >= s - 1, u, d), up_pairs + down_pairs)
                up[p].append(both)
                down[p].append(both)
            else:
                up[p].append(hop(u, up_pairs))
                down[p].append(hop(d, down_pairs))

    hid = hbm(jnp.concatenate([hidden, swap(hidden)]))
    hid_t = turn_call(hid, tile)
    tgt = mine(logits, True)
    tgt = swap(tgt)
    local = jnp.concatenate([ids, swap(ids)]) - (voc * share + core * half)
    e_t, t_stat = target_call(scalar(core), logits, tgt, local[:, None], tile)

    stats, e_z = [], []
    whole = [gathered(up, down, p, nz) for p in range(PARTS)]
    for p in range(PARTS):
        outs = last_call(p, nz, scalar(z), whole[p], hid, e_t, t_stat, stats, tile)
        e_z.append(outs[0])
        if p < PARTS - 1:
            stats.append(outs[1])
    mine_rows, turned, tops = outs[1:]

    x = fold_rows(mine_rows, swap(turned))
    bits = n_voc.bit_length() - 1
    done = 0
    while True:
        few = min(2, bits - done)
        got = [x] + [plane_swap(x, v << done) for v in range(1, 1 << few)]
        done += few
        if done >= bits:
            break
        while len(got) > 1:
            got = [fold_rows(got[j], got[j + 1]) for j in range(0, len(got), 2)]
        x = got[0]

    def first_row(s):
        return jnp.where(z < s, jnp.minimum(z + nz - s, nz - 1), jnp.maximum(z - nz + s, 0))

    msgs, slope = [], []
    for p in range(PARTS):
        head_args = got + [tops] if p == 0 else [coef]
        outs = slope_call(
            p, scalar(first_row(1)), head_args, e_z[p], e_t, hid_t, deep, wide
        )
        slope.append(outs[0])
        msgs.append(outs[1])
        if p == 0:
            coef, plane = outs[2:]

    def grad_rows(index, p):
        return dot(lax.dynamic_slice_in_dim(hid_t, index * deep, deep, 0), slope[p])

    got_up, got_down = [None] * PARTS, [None] * PARTS
    for s in range(1, nz):
        up_pairs = [(a, a + 1) for a in range(0, s)]
        down_pairs = [(a, a - 1) for a in range(nz - s, nz)]
        for p in range(PARTS):
            if 2 * s <= nz:
                if s == 1:
                    msg = msgs[p]
                else:
                    msg = grad_rows(first_row(s), p) + got_up[p].astype(f32)
                    if got_down[p] is not got_up[p]:
                        msg = msg + got_down[p].astype(f32)
                    msg = msg.astype(bf16)
                if 2 * s < nz - 1:
                    got_up[p] = got_down[p] = hop(msg, up_pairs + down_pairs)
                else:
                    got_up[p] = hop(msg, up_pairs)
                    got_down[p] = hop(msg, down_pairs)
            else:
                msg_up = grad_rows(jnp.minimum(z + nz - s, nz - 1), p) + got_up[p].astype(f32)
                msg_down = grad_rows(jnp.maximum(z - nz + s, 0), p) + got_down[p].astype(f32)
                got_up[p] = hop(msg_up.astype(bf16), up_pairs)
                got_down[p] = hop(msg_down.astype(bf16), down_pairs)
    keeps, gives = [], []
    for p in range(PARTS):
        full = grad_rows(z, p) + got_up[p].astype(f32) + got_down[p].astype(f32)
        low, high = full[:own_rows], full[own_rows:]
        keeps.append(jnp.where(core == 0, low, high))
        give = jnp.where(core == 0, high, low).astype(bf16)
        gives.append(swap(give).astype(f32))
    grad_head = jnp.where(
        core == 0,
        jnp.concatenate(keeps + gives, axis=1),
        jnp.concatenate(gives + keeps, axis=1),
    )

    late, plane, _ = lax.optimization_barrier((slope, plane, msgs[-1]))
    planes = [hop(plane, [(a, (a + k) % nz) for a in range(nz)]) for k in range(1, nz)]
    planes, _ = lax.optimization_barrier(([plane] + planes, got_up[0]))
    spot = lax.broadcasted_iota(jnp.int32, (nz, 1), 0)
    every = jnp.zeros((nz, 1), f32)
    for k in range(nz):
        every = jnp.where(spot == lax.rem(z - k + nz, nz), planes[k][:1, :1], every)
    loss = jnp.sum(every) / (rows * n_tok)

    part = hidden_call(nz, scalar(z), late, whole, dh, tile)
    part = part[:rows].astype(f32) + swap(part[rows:]).astype(f32)
    width = dh // n_voc

    def wide_slice(w):
        return lax.dynamic_slice_in_dim(part, w * width, width, 1)

    grad_hidden = wide_slice(voc)
    for v in range(1, n_voc):
        came = plane_swap(wide_slice(voc ^ v).astype(bf16), v)
        grad_hidden = grad_hidden + came.astype(f32)
    return loss, grad_hidden, grad_head


def solution(mesh):
    placed = (P("tok", None), P("tok", "voc"), P("tok", "voc"), P("tok"))
    n_tok, n_voc = mesh.shape["tok"], mesh.shape["voc"]
    return jax.shard_map(
        functools.partial(body, n_tok, n_voc),
        mesh=mesh,
        in_specs=placed,
        out_specs=(P(), P("tok", "voc"), P("tok", "voc")),
        check_vma=False,
    )
```

```python
import functools
import jax
import jax.numpy as jnp
from jax import lax
from jax.experimental import pallas as pl
from jax.experimental.pallas import tpu as pltpu
from jax.sharding import PartitionSpec as P


ce_weight = 0.5
PARTS = 2
f32, bf16 = jnp.float32, jnp.bfloat16


def dot(a, b):
    return lax.dot_general(a, b, (((1,), (0,)), ((), ())), preferred_element_type=f32)


def dot_nt(a, b):
    return lax.dot_general(a, b, (((1,), (1,)), ((), ())), preferred_element_type=f32)


def lanes(columns, like):
    lane = lax.broadcasted_iota(jnp.int32, like, 1)
    out = jnp.zeros(like, f32)
    for k, c in enumerate(columns):
        out = jnp.where(lane == k, c, out)
    return out


def cost(flops, size, trans=0):
    return pl.CostEstimate(flops=flops, bytes_accessed=size, transcendentals=trans)


WHOLE = pl.BlockSpec(memory_space=pltpu.VMEM)


def near(x):
    return pltpu.with_memory_space_constraint(x, pltpu.VMEM)


def out(shape, dtype):
    return pltpu.VMEM(shape, dtype)


def params(size):
    return pltpu.CompilerParams(vmem_limit_bytes=size << 20)


def target_kernel(own_tiles, core_ref, mine_ref, came_ref, id_ref, e_ref, stat_ref):
    step = pl.program_id(0)
    t = jnp.where(step < own_tiles, mine_ref[...], came_ref[...]).astype(f32)
    at = pl.ds(pl.multiple_of(step * t.shape[0], t.shape[0]), t.shape[0])
    top = jnp.max(t, axis=1, keepdims=True)
    e = jnp.exp(t - top)
    e_ref[at, :] = e.astype(bf16)
    total = jnp.sum(e, axis=1, keepdims=True)
    first = jnp.sum(e * t, axis=1, keepdims=True)
    ids = id_ref[...].astype(f32)
    stat_ref[at, :] = lanes([top, total, first, ids], (t.shape[0], 128))


def target_call(core, logits, came, ids, tile):
    rows, half = came.shape
    n, own_tiles = 2 * rows, rows // tile
    return pl.pallas_call(
        functools.partial(target_kernel, own_tiles),
        grid_spec=pltpu.PrefetchScalarGridSpec(
            num_scalar_prefetch=1,
            grid=(n // tile,),
            in_specs=[
                pl.BlockSpec((tile, half), lambda i, s: (jnp.minimum(i, own_tiles - 1), s[0])),
                pl.BlockSpec((tile, half), lambda i, s: (jnp.maximum(i - own_tiles, 0), 0)),
                pl.BlockSpec((tile, 1), lambda i, s: (i, 0)),
            ],
            out_specs=[WHOLE, WHOLE],
        ),
        out_shape=[out((n, half), bf16), out((n, 128), f32)],
        compiler_params=params(16),
        cost_estimate=cost(8 * n * half, 4 * n * half, n * half),
        name="target_exps",
    )(core, logits, came, ids)


def turn_kernel(tile, x_ref, out_ref):
    for k in range(x_ref.shape[0] // tile):
        at = slice(k * tile, (k + 1) * tile)
        out_ref[:, at] = x_ref[at, :].T


def turn_call(x, tile):
    n, dh = x.shape
    return pl.pallas_call(
        functools.partial(turn_kernel, tile),
        in_specs=[WHOLE],
        out_specs=WHOLE,
        out_shape=out((dh, n), bf16),
        compiler_params=params(8),
        cost_estimate=cost(0, 4 * n * dh),
        name="turn",
    )(near(x))


def choices(nz):
    unique, table = [("own", 0)], []
    for j in range(1, nz):
        table.append((("down", j), ("up", nz - j)))
        unique += [c for c in table[-1] if c not in unique]
    return unique, table


def gathered(up, down, p, nz, all_steps):
    unique, _ = choices(nz)
    pick = {"own": up, "up": up, "down": down}
    return [pick[k][p][j] for k, j in unique if all_steps or j < nz - 1]


def assemble(z, nz, refs, whole_ref, sem):
    unique, table = choices(nz)
    if len(refs) < len(unique):
        unique = [c for c in unique if c[1] < nz - 1]
    deep = refs[0].shape[0]

    def place(j):
        return pl.ds(pl.multiple_of(lax.rem(z + j, nz) * deep, deep), deep)

    def copy(k, j):
        return pltpu.make_async_copy(refs[k], whole_ref.at[place(j), :], sem.at[j])

    def each(do):
        do(0, 0)
        for j in range(1, nz):
            for choice, here in zip(table[j - 1], (z + j < nz, z + j >= nz)):

                @pl.when(here)
                def _(choice=choice, j=j):
                    if choice in unique:
                        do(unique.index(choice), j)
                    else:
                        do(None, j)

    def start(k, j):
        if k is None:
            whole_ref[place(j), :] = jnp.zeros((deep, whole_ref.shape[1]), bf16)
        else:
            copy(k, j).start()

    def wait(k, j):
        if k is not None:
            copy(k, j).wait()

    each(start)
    return lambda: each(wait)


def early_kernel(nz, count, z_ref, *refs):
    w_refs = refs[:count]
    h_ref, acc_ref, whole_ref, sem = refs[count:]

    @pl.when(pl.program_id(0) == 0)
    def _():
        assemble(z_ref[0], nz, w_refs, whole_ref, sem)()

    tile = h_ref.shape[0] // pl.num_programs(0)
    at = pl.ds(pl.multiple_of(pl.program_id(0) * tile, tile), tile)
    acc_ref[at, :] = dot(h_ref[at, :], whole_ref[...])


def early_call(nz, z, blocks, hid, tile):
    n, dh = hid.shape
    piece = blocks[0].shape[1]
    return pl.pallas_call(
        functools.partial(early_kernel, nz, len(blocks)),
        grid_spec=pltpu.PrefetchScalarGridSpec(
            num_scalar_prefetch=1,
            grid=(n // tile,),
            in_specs=[pl.BlockSpec(memory_space=pl.ANY)] * len(blocks) + [WHOLE],
            out_specs=WHOLE,
            scratch_shapes=[pltpu.VMEM((dh, piece), bf16), pltpu.SemaphoreType.DMA((nz,))],
        ),
        out_shape=out((n, piece), f32),
        compiler_params=params(10),
        cost_estimate=cost(2 * n * dh * piece, 6 * n * piece),
        name="early_draft",
    )(z, *blocks, near(hid))


def last_kernel(part, earlier, tile, at_ref, *refs):
    w_ref, acc_ref, h_ref, e_ref, t_ref = refs[:5]
    stat_refs = refs[5:5 + earlier]
    outs = refs[5 + earlier:]
    n, piece = acc_ref.shape
    deep = w_ref.shape[0]
    block = pl.ds(pl.multiple_of(at_ref[0] * deep, deep), deep)
    like = (tile, 128)
    for k in range(n // tile):
        at = slice(k * tile, (k + 1) * tile)
        z = acc_ref[at, :] + dot(h_ref[at, block], w_ref[...])
        top = jnp.max(z, axis=1, keepdims=True)
        e = jnp.exp(z - top)
        outs[0][at, :] = e.astype(bf16)
        total = jnp.sum(e, axis=1, keepdims=True)
        e_t = e_ref[at, part * piece:(part + 1) * piece].astype(f32)
        cross = jnp.sum(e_t * z, axis=1, keepdims=True)
        t_stat = t_ref[at, :]
        column = lax.broadcasted_iota(jnp.int32, z.shape, 1) + part * piece
        id_col = t_stat[:, 3:4].astype(jnp.int32)
        own = jnp.sum(jnp.where(column == id_col, z, 0.0), axis=1, keepdims=True)
        if part < PARTS - 1:
            outs[1][at, :] = lanes([top, total, cross, own], like)
            continue
        send_ref, turn_ref, tops_ref = outs[1:]
        stats = [r[at, :] for r in stat_refs]
        all_top = top
        for r in stats:
            all_top = jnp.maximum(all_top, r[:, 0:1])
        total = total * jnp.exp(top - all_top)
        for r in stats:
            total = total + r[:, 1:2] * jnp.exp(r[:, 0:1] - all_top)
            cross = cross + r[:, 2:3]
            own = own + r[:, 3:4]
        t_top, t_total, t_first = t_stat[:, 0:1], t_stat[:, 1:2], t_stat[:, 2:3]
        rows = lanes([t_top, t_total, t_first - cross, all_top, total, own], like).T[:8]
        send_ref[:, at] = rows
        turned = (k * tile + n // 2) % n
        turn_ref[:, turned:turned + tile] = rows
        tops = [r[:, 0:1] for r in stats] + [top]
        tops_ref[at, :] = lanes([t_top] + tops + [t_stat[:, 3:4]], like)


def last_call(part, at, w, acc, hid, e_t, t_stat, stats, tile):
    n, piece = acc.shape
    out_shape = [out((n, piece), bf16)]
    if part < PARTS - 1:
        stats = []
        out_shape += [out((n, 128), f32)]
    else:
        out_shape += [out((8, n), f32), out((8, n), f32), out((n, 128), f32)]
    return pl.pallas_call(
        functools.partial(last_kernel, part, len(stats), tile),
        grid_spec=pltpu.PrefetchScalarGridSpec(
            num_scalar_prefetch=1,
            grid=(1,),
            in_specs=[WHOLE] * (5 + len(stats)),
            out_specs=[WHOLE] * len(out_shape),
        ),
        out_shape=out_shape,
        compiler_params=params(10),
        cost_estimate=cost(2 * n * w.shape[0] * piece, 8 * n * piece, n * piece),
        name="last_draft",
    )(at, near(w), near(acc), near(hid), near(e_t), near(t_stat), *map(near, stats))


def hidden_kernel(nz, count, z_ref, *refs):
    slope_refs, w_refs = refs[:PARTS], refs[PARTS:PARTS + PARTS * count]
    out_ref, whole_ref, sem = refs[PARTS + PARTS * count:]

    @pl.when(pl.program_id(0) == 0)
    def _():
        waits = [
            assemble(z_ref[0], nz, w_refs[p * count:(p + 1) * count], whole_ref.at[p], sem.at[p])
            for p in range(PARTS)
        ]
        for wait in waits:
            wait()

    tile = out_ref.shape[0]
    at = pl.ds(pl.multiple_of(pl.program_id(0) * tile, tile), tile)
    acc = dot_nt(slope_refs[0][at, :], whole_ref[0])
    for p in range(1, PARTS):
        acc = acc + dot_nt(slope_refs[p][at, :], whole_ref[p])
    out_ref[...] = acc.astype(bf16)


def hidden_call(nz, z, slope, blocks, dh, tile):
    n, piece = slope[0].shape
    count = len(blocks[0])
    row = lambda i, s: (i, 0)
    return pl.pallas_call(
        functools.partial(hidden_kernel, nz, count),
        grid_spec=pltpu.PrefetchScalarGridSpec(
            num_scalar_prefetch=1,
            grid=(n // tile,),
            in_specs=[WHOLE] * PARTS
            + [pl.BlockSpec(memory_space=pl.ANY)] * (PARTS * count),
            out_specs=pl.BlockSpec((tile, dh), row),
            scratch_shapes=[
                pltpu.VMEM((PARTS, dh, piece), bf16),
                pltpu.SemaphoreType.DMA((PARTS, nz)),
            ],
        ),
        out_shape=jax.ShapeDtypeStruct((n, dh), bf16),
        compiler_params=params(16),
        cost_estimate=cost(2 * n * dh * piece * PARTS, 8 * n * piece),
        name="hidden_grad",
    )(z, *map(near, slope), *[b for bs in blocks for b in bs])


def fold_rows(a, b):
    t_top = jnp.maximum(a[0:1], b[0:1])
    fa, fb = jnp.exp(a[0:1] - t_top), jnp.exp(b[0:1] - t_top)
    z_top = jnp.maximum(a[3:4], b[3:4])
    ga, gb = jnp.exp(a[3:4] - z_top), jnp.exp(b[3:4] - z_top)
    rows = [
        t_top,
        a[1:2] * fa + b[1:2] * fb,
        a[2:3] * fa + b[2:3] * fb,
        z_top,
        a[4:5] * ga + b[4:5] * gb,
        a[5:6] + b[5:6],
    ]
    return jnp.concatenate(rows + [a[6:8]])


def fold_kernel(*refs):
    got = [r[...] for r in refs[:-1]]
    while len(got) > 1:
        got = [fold_rows(got[j], got[j + 1]) for j in range(0, len(got), 2)]
    refs[-1][...] = got[0]


def fold_call(rows):
    return pl.pallas_call(
        fold_kernel,
        in_specs=[WHOLE] * len(rows),
        out_specs=WHOLE,
        out_shape=out(rows[0].shape, f32),
        compiler_params=params(4),
        name="fold",
    )(*map(near, rows))


def slope_kernel(part, peers, idx_ref, *refs):
    step = pl.program_id(0)
    if peers:
        tops_ref = refs[peers]
        ez_ref, et_ref, ht_ref = refs[peers + 1:peers + 4]
        slope_ref, msg_ref, coef_ref, loss_ref = refs[peers + 4:]

        @pl.when(step == 0)
        def _():
            got = [r[...] for r in refs[:peers]]
            while len(got) > 1:
                got = [fold_rows(got[j], got[j + 1]) for j in range(0, len(got), 2)]
            s = got[0]
            t_inv = 1.0 / s[1:2]
            lse_t = s[0:1] + jnp.log(s[1:2])
            lse_z = s[3:4] + jnp.log(s[4:5])
            n = s.shape[1]
            per_token = s[2:3] * t_inv - lse_t + (1.0 + ce_weight) * lse_z - ce_weight * s[5:6]
            plane = jnp.sum(per_token[:, :n // 2], axis=1, keepdims=True) + jnp.sum(
                per_token[:, n // 2:], axis=1, keepdims=True
            )
            loss_ref[...] = jnp.broadcast_to(plane, loss_ref.shape)
            z_inv = (1.0 + ce_weight) / s[4:5]
            flat = jnp.concatenate([s[0:1], t_inv, s[3:4], z_inv, jnp.zeros((124, n), f32)]).T
            tops = tops_ref[...]
            lane = lax.broadcasted_iota(jnp.int32, tops.shape, 1)
            base = jnp.where(lane == 0, flat[:, 0:1], flat[:, 2:3])
            gain = jnp.where(lane == 0, flat[:, 1:2], flat[:, 3:4])
            coef_ref[...] = jnp.where(lane <= PARTS, jnp.exp(tops - base) * gain, tops)

    else:
        coef_ref, ez_ref, et_ref, ht_ref, slope_ref, msg_ref = refs
    b = coef_ref[:, 0:1]
    a = coef_ref[:, part + 1:part + 2]
    piece = ez_ref.shape[1]
    tile = piece // pl.num_programs(0)
    first = pl.multiple_of(step * tile, tile)
    at = pl.ds(first, tile)
    e_t = et_ref[:, pl.ds(pl.multiple_of(part * piece + first, tile), tile)]
    value = ez_ref[:, at].astype(f32) * a - e_t.astype(f32) * b
    column = lax.broadcasted_iota(jnp.int32, value.shape, 1)
    id_col = coef_ref[:, PARTS + 1:PARTS + 2].astype(jnp.int32) - (part * piece + first)
    value = jnp.where(column == id_col, value - ce_weight, value)
    slope = value.astype(bf16)
    slope_ref[:, at] = slope
    deep = msg_ref.shape[0]
    rows = pl.ds(pl.multiple_of(idx_ref[0] * deep, deep), deep)
    msg_ref[...] = dot(ht_ref[rows, :], slope).astype(bf16)


def slope_call(part, index, head_args, e_z, e_t, hid_t, deep, tile):
    n, piece = e_z.shape
    peers = len(head_args) - 1
    out_specs = [WHOLE, pl.BlockSpec((deep, tile), lambda i, s: (0, i))]
    out_shape = [out((n, piece), bf16), jax.ShapeDtypeStruct((deep, piece), bf16)]
    if peers:
        out_specs += [WHOLE, WHOLE]
        out_shape += [out((n, 128), f32), out((8, 128), f32)]
    args = [*head_args, e_z, e_t, hid_t]
    return pl.pallas_call(
        functools.partial(slope_kernel, part, peers),
        grid_spec=pltpu.PrefetchScalarGridSpec(
            num_scalar_prefetch=1,
            grid=(piece // tile,),
            in_specs=[WHOLE] * len(args),
            out_specs=out_specs,
        ),
        out_shape=out_shape,
        compiler_params=params(16),
        cost_estimate=cost(2 * n * deep * piece, 6 * n * piece),
        name="slope",
    )(index, *map(near, args))


def loss_kernel(scale, z_ref, *refs):
    planes, out_ref = [r[...] for r in refs[:-1]], refs[-1]
    nz = len(planes)
    total = jnp.zeros(out_ref.shape, f32)
    for chip in range(nz):
        k = lax.rem(z_ref[0] - chip + nz, nz)
        term = planes[0]
        for j in range(1, nz):
            term = jnp.where(k == j, planes[j], term)
        total = total + term
    out_ref[...] = total * scale


def loss_call(z, planes, scale):
    return pl.pallas_call(
        functools.partial(loss_kernel, scale),
        grid_spec=pltpu.PrefetchScalarGridSpec(
            num_scalar_prefetch=1,
            grid=(1,),
            in_specs=[WHOLE] * len(planes),
            out_specs=WHOLE,
        ),
        out_shape=jax.ShapeDtypeStruct(planes[0].shape, f32),
        compiler_params=params(4),
        name="loss_sum",
    )(z, *planes)


def body(n_tok, n_voc, hidden, head, logits, ids):
    nz = n_tok // 2
    rows, dh = hidden.shape
    own_rows, share = head.shape
    half = share // 2
    piece = half // PARTS
    deep = 2 * own_rows
    tile = min(256, rows)
    wide = min(512, piece)
    me = lax.axis_index("tok")
    core = lax.rem(me, 2)
    z = lax.div(me, 2)
    voc = lax.axis_index("voc")
    width = dh // n_voc

    def first_row(s):
        return jnp.where(z < s, jnp.minimum(z + nz - s, nz - 1), jnp.maximum(z - nz + s, 0))

    def scalar(x):
        return jnp.reshape(x, (1,)).astype(jnp.int32)

    even = core == 0
    above = [z >= s for s in range(nz)]
    ahead = {
        "core": scalar(core),
        "z": scalar(z),
        "last": scalar(jnp.where(z == 0, nz - 1, 0)),
        "first": scalar(first_row(1)),
    }
    row_of = {("own", 0): z * deep}
    for s in range(1, nz):
        if 2 * s <= nz:
            row_of["first", s] = first_row(s) * deep
        row_of["up", s] = jnp.minimum(z + nz - s, nz - 1) * deep
        row_of["down", s] = jnp.maximum(z - nz + s, 0) * deep
    col_of = [(voc ^ v) * width for v in range(n_voc)]
    vocab_start = voc * share + core * half
    (even, above, ahead, row_of, col_of, vocab_start), head, hidden, logits, ids = (
        lax.optimization_barrier(
            ((even, above, ahead, row_of, col_of, vocab_start), head, hidden, logits, ids)
        )
    )

    def swap(x):
        return lax.ppermute(x, "tok", [(i, i ^ 1) for i in range(n_tok)])

    def hop(x, pairs):
        return lax.ppermute(x, "tok", [(2 * a + k, 2 * b + k) for a, b in pairs for k in range(2)])

    def plane_swap(x, v):
        return lax.ppermute(x, "voc", [(w, w ^ v) for w in range(n_voc)])

    def mine(x, other=False):
        left, right = x[:, :half], x[:, half:]
        return jnp.where(even, right, left) if other else jnp.where(even, left, right)

    keep, send = mine(head), mine(head, True)
    blocks = []
    for p in range(PARTS):
        cut = slice(p * piece, (p + 1) * piece)
        other = swap(send[:, cut])
        blocks.append(
            jnp.where(
                even,
                jnp.concatenate([keep[:, cut], other]),
                jnp.concatenate([other, keep[:, cut]]),
            )
        )

    up = [[b] for b in blocks]
    down = [[b] for b in blocks]
    for s in range(1, nz):
        up_pairs = [(a, a + 1) for a in range(s - 1, nz - 1)]
        down_pairs = [(a, a - 1) for a in range(1, nz - s + 1)]
        for p in range(PARTS):
            u, d = up[p][-1], down[p][-1]
            if 2 * s > nz + 1:
                both = hop(jnp.where(above[s - 1], u, d), up_pairs + down_pairs)
                up[p].append(both)
                down[p].append(both)
            else:
                up[p].append(hop(u, up_pairs))
                down[p].append(hop(d, down_pairs))

    hid = jnp.concatenate([hidden, swap(hidden)])
    hid_t = turn_call(hid, tile)
    tgt = mine(logits, True)
    tgt = swap(tgt)
    local = jnp.concatenate([ids, swap(ids)]) - vocab_start
    e_t, t_stat = target_call(ahead["core"], logits, tgt, local[:, None], tile)

    stats, e_z = [], []
    whole = [gathered(up, down, p, nz, True) for p in range(PARTS)]
    for p in range(PARTS):
        acc = early_call(nz, ahead["z"], gathered(up, down, p, nz, False), hid, tile)
        final_u, final_d = up[p][-1], down[p][-1]
        w = final_u if final_u is final_d else jnp.where(above[nz - 1], final_u, final_d)
        outs = last_call(p, ahead["last"], w, acc, hid, e_t, t_stat, stats, tile)
        e_z.append(outs[0])
        if p < PARTS - 1:
            stats.append(outs[1])
    mine_rows, turned, tops = outs[1:]

    x = fold_call([mine_rows, swap(turned)])
    bits = n_voc.bit_length() - 1
    done = 0
    while True:
        few = min(2, bits - done)
        got = [x] + [plane_swap(x, v << done) for v in range(1, 1 << few)]
        done += few
        if done >= bits:
            break
        x = fold_call(got)

    msgs, slope = [], []
    for p in range(PARTS):
        head_args = got + [tops] if p == 0 else [coef]
        outs = slope_call(
            p, ahead["first"], head_args, e_z[p], e_t, hid_t, deep, wide
        )
        slope.append(outs[0])
        msgs.append(outs[1])
        if p == 0:
            coef, plane = outs[2:]

    def cut(x, row, col, shape):
        row, col = (jnp.asarray(i, jnp.int32) for i in (row, col))
        return lax.dynamic_slice(x, (row, col), shape, allow_negative_indices=False)

    def grad_rows(way, s, p):
        return dot(cut(hid_t, row_of[way, s], 0, (deep, 2 * rows)), slope[p])

    got_up, got_down = [None] * PARTS, [None] * PARTS
    for s in range(1, nz):
        up_pairs = [(a, a + 1) for a in range(0, s)]
        down_pairs = [(a, a - 1) for a in range(nz - s, nz)]
        for p in range(PARTS):
            if 2 * s <= nz:
                if s == 1:
                    msg = msgs[p]
                else:
                    msg = grad_rows("first", s, p) + got_up[p].astype(f32)
                    if got_down[p] is not got_up[p]:
                        msg = msg + got_down[p].astype(f32)
                    msg = msg.astype(bf16)
                if 2 * s < nz - 1:
                    got_up[p] = got_down[p] = hop(msg, up_pairs + down_pairs)
                else:
                    got_up[p] = hop(msg, up_pairs)
                    got_down[p] = hop(msg, down_pairs)
            else:
                msg_up = grad_rows("up", s, p) + got_up[p].astype(f32)
                msg_down = grad_rows("down", s, p) + got_down[p].astype(f32)
                got_up[p] = hop(msg_up.astype(bf16), up_pairs)
                got_down[p] = hop(msg_down.astype(bf16), down_pairs)
    keeps, gives = [], []
    for p in range(PARTS):
        full = grad_rows("own", 0, p) + got_up[p].astype(f32) + got_down[p].astype(f32)
        low, high = full[:own_rows], full[own_rows:]
        keeps.append(jnp.where(even, low, high))
        give = jnp.where(even, high, low).astype(bf16)
        gives.append(swap(give).astype(f32))
    grad_head = jnp.where(
        even,
        jnp.concatenate(keeps + gives, axis=1),
        jnp.concatenate(gives + keeps, axis=1),
    )

    late, plane, _ = lax.optimization_barrier((slope, plane, msgs[-1]))
    planes = [hop(plane, [(a, (a + k) % nz) for a in range(nz)]) for k in range(1, nz)]
    loss = loss_call(ahead["z"], [plane] + planes, 1.0 / (rows * n_tok))[0, 0]

    part = hidden_call(nz, ahead["z"], late, whole, dh, tile)
    part = part[:rows].astype(f32) + swap(part[rows:]).astype(f32)

    def wide_slice(v):
        return cut(part, 0, col_of[v], (rows, width))

    grad_hidden = wide_slice(0)
    for v in range(1, n_voc):
        came = plane_swap(wide_slice(v).astype(bf16), v)
        grad_hidden = grad_hidden + came.astype(f32)
    return loss, grad_hidden, grad_head


def solution(mesh):
    placed = (P("tok", None), P("tok", "voc"), P("tok", "voc"), P("tok"))
    n_tok, n_voc = mesh.shape["tok"], mesh.shape["voc"]
    return jax.shard_map(
        functools.partial(body, n_tok, n_voc),
        mesh=mesh,
        in_specs=placed,
        out_specs=(P(), P("tok", "voc"), P("tok", "voc")),
        check_vma=False,
    )
```

```python
import functools
import jax
import jax.numpy as jnp
from jax import lax
from jax.experimental import pallas as pl
from jax.experimental.pallas import tpu as pltpu
from jax.sharding import PartitionSpec as P


ce_weight = 0.5
PARTS = 2
f32, bf16 = jnp.float32, jnp.bfloat16


def dot(a, b):
    return lax.dot_general(a, b, (((1,), (0,)), ((), ())), preferred_element_type=f32)


def dot_nt(a, b):
    return lax.dot_general(a, b, (((1,), (1,)), ((), ())), preferred_element_type=f32)


def lanes(columns, like, first=0):
    lane = lax.broadcasted_iota(jnp.int32, like, 1)
    out = jnp.zeros(like, f32)
    for k, c in enumerate(columns):
        out = jnp.where(lane == first + k, c, out)
    return out


def block_of(kind, z, s):
    ahead = (z % 2 == 0) == (kind == "even")
    return z + s if ahead else z - s


def edge(kind, z):
    return z ^ 1 if kind == "even" else ((z + 1) ^ 1) - 1


def holders(kind, nz, s):
    return [z for z in range(nz) if 0 <= block_of(kind, z, s) < nz]


def arrivals(nz):
    return [("own", 0)] + [
        (kind, s) for s in range(1, nz) for kind in ("even", "odd") if holders(kind, nz, s)
    ]


def cost(flops, size, trans=0):
    return pl.CostEstimate(flops=flops, bytes_accessed=size, transcendentals=trans)


WHOLE = pl.BlockSpec(memory_space=pltpu.VMEM)


def near(x):
    return pltpu.with_memory_space_constraint(x, pltpu.VMEM)


def out(shape, dtype):
    return pltpu.VMEM(shape, dtype)


def params(size):
    return pltpu.CompilerParams(vmem_limit_bytes=size << 20)


def target_kernel(own_tiles, core_ref, mine_ref, came_ref, id_ref, e_ref, stat_ref):
    step = pl.program_id(0)
    t = jnp.where(step < own_tiles, mine_ref[...], came_ref[...]).astype(f32)
    at = pl.ds(pl.multiple_of(step * t.shape[0], t.shape[0]), t.shape[0])
    top = jnp.max(t, axis=1, keepdims=True)
    e = jnp.exp(t - top)
    e_ref[at, :] = e.astype(bf16)
    total = jnp.sum(e, axis=1, keepdims=True)
    first = jnp.sum(e * t, axis=1, keepdims=True)
    ids = id_ref[...].astype(f32)
    stat_ref[at, :] = lanes([top, total, first, ids], (t.shape[0], 128))


def target_call(core, logits, came, ids, tile):
    rows, half = came.shape
    n, own_tiles = 2 * rows, rows // tile
    return pl.pallas_call(
        functools.partial(target_kernel, own_tiles),
        grid_spec=pltpu.PrefetchScalarGridSpec(
            num_scalar_prefetch=1,
            grid=(n // tile,),
            in_specs=[
                pl.BlockSpec((tile, half), lambda i, s: (jnp.minimum(i, own_tiles - 1), s[0])),
                pl.BlockSpec((tile, half), lambda i, s: (jnp.maximum(i - own_tiles, 0), 0)),
                pl.BlockSpec((tile, 1), lambda i, s: (i, 0)),
            ],
            out_specs=[WHOLE, WHOLE],
        ),
        out_shape=[out((n, half), bf16), out((n, 128), f32)],
        compiler_params=params(16),
        cost_estimate=cost(8 * n * half, 4 * n * half, n * half),
        name="target_exps",
    )(core, logits, came, ids)


def turn_kernel(tile, x_ref, out_ref):
    for k in range(x_ref.shape[0] // tile):
        at = slice(k * tile, (k + 1) * tile)
        out_ref[:, at] = x_ref[at, :].T


def turn_call(x, tile):
    n, dh = x.shape
    return pl.pallas_call(
        functools.partial(turn_kernel, tile),
        in_specs=[WHOLE],
        out_specs=WHOLE,
        out_shape=out((dh, n), bf16),
        compiler_params=params(8),
        cost_estimate=cost(0, 4 * n * dh),
        name="turn",
    )(near(x))


def assemble(z, nz, count, refs, whole_ref, sem):
    deep = refs[0].shape[0]
    given = arrivals(nz)[:count]

    def place(block):
        return pl.ds(pl.multiple_of(block * deep, deep), deep)

    def each(act):
        for k, (kind, s) in enumerate(given):
            if kind == "own":
                act(k, z)
                continue
            sign = jnp.where((lax.rem(z, 2) == 0) == (kind == "even"), 1, -1)
            block = z + sign * s

            @pl.when(jnp.logical_and(block >= 0, block < nz))
            def _(k=k, block=block):
                act(k, block)

    def copy(k, block):
        return pltpu.make_async_copy(refs[k], whole_ref.at[place(block), :], sem.at[k])

    each(lambda k, block: copy(k, block).start())
    if count < len(arrivals(nz)):

        @pl.when(jnp.logical_or(z == 0, z == nz - 1))
        def _():
            hole = jnp.where(z == 0, nz - 1, 0)
            whole_ref[place(hole), :] = jnp.zeros((deep, whole_ref.shape[1]), bf16)

    return lambda: each(lambda k, block: copy(k, block).wait())


def early_kernel(nz, count, z_ref, *refs):
    w_refs = refs[:count]
    h_ref, acc_ref, whole_ref, sem = refs[count:]

    @pl.when(pl.program_id(0) == 0)
    def _():
        assemble(z_ref[0], nz, count, w_refs, whole_ref, sem)()

    tile = h_ref.shape[0] // pl.num_programs(0)
    at = pl.ds(pl.multiple_of(pl.program_id(0) * tile, tile), tile)
    acc_ref[at, :] = dot(h_ref[at, :], whole_ref[...])


def early_call(nz, z, blocks, hid, tile):
    n, dh = hid.shape
    piece = blocks[0].shape[1]
    return pl.pallas_call(
        functools.partial(early_kernel, nz, len(blocks)),
        grid_spec=pltpu.PrefetchScalarGridSpec(
            num_scalar_prefetch=1,
            grid=(n // tile,),
            in_specs=[pl.BlockSpec(memory_space=pl.ANY)] * len(blocks) + [WHOLE],
            out_specs=WHOLE,
            scratch_shapes=[
                pltpu.VMEM((dh, piece), bf16),
                pltpu.SemaphoreType.DMA((len(blocks),)),
            ],
        ),
        out_shape=out((n, piece), f32),
        compiler_params=params(10),
        cost_estimate=cost(2 * n * dh * piece, 6 * n * piece),
        name="early_draft",
    )(z, *blocks, near(hid))


def last_kernel(part, earlier, tile, at_ref, *refs):
    w_ref, acc_ref, h_ref, e_ref, t_ref = refs[:5]
    stat_refs = refs[5:5 + earlier]
    outs = refs[5 + earlier:]
    n, piece = acc_ref.shape
    deep = w_ref.shape[0]
    block = pl.ds(pl.multiple_of(at_ref[0] * deep, deep), deep)
    like = (tile, 128)
    for k in range(n // tile):
        at = slice(k * tile, (k + 1) * tile)
        z = acc_ref[at, :] + dot(h_ref[at, block], w_ref[...])
        top = jnp.max(z, axis=1, keepdims=True)
        e = jnp.exp(z - top)
        outs[0][at, :] = e.astype(bf16)
        total = jnp.sum(e, axis=1, keepdims=True)
        e_t = e_ref[at, part * piece:(part + 1) * piece].astype(f32)
        cross = jnp.sum(e_t * z, axis=1, keepdims=True)
        t_stat = t_ref[at, :]
        column = lax.broadcasted_iota(jnp.int32, z.shape, 1) + part * piece
        id_col = t_stat[:, 3:4].astype(jnp.int32)
        own = jnp.sum(jnp.where(column == id_col, z, 0.0), axis=1, keepdims=True)
        stat = lanes([top, total, cross, own], like, 4 + 4 * part)
        if part < PARTS - 1:
            outs[1][at, :] = stat
            continue
        send_ref, turn_ref, tops_ref = outs[1:]
        stat = stat + t_stat
        for r in stat_refs:
            stat = stat + r[at, :]
        row = stat.T
        row = [row[k:k + 1] for k in range(4 + 4 * PARTS)]
        tops = row[4::4]
        all_top = functools.reduce(jnp.maximum, tops)
        total = sum(row[5 + 4 * p] * jnp.exp(tops[p] - all_top) for p in range(PARTS))
        cross, own = sum(row[6::4]), sum(row[7::4])
        blank = jnp.zeros((1, tile), f32)
        rows = [row[0], row[1], row[2] - cross, all_top, total, own, blank, blank]
        rows = jnp.concatenate(rows)
        send_ref[:, at] = rows
        turned = (k * tile + n // 2) % n
        turn_ref[:, turned:turned + tile] = rows
        tops = [row[0]] + tops + [row[3]]
        tops_ref[:, at] = jnp.concatenate(tops + [blank] * (8 - len(tops)))


def last_call(part, at, w, acc, hid, e_t, t_stat, stats, tile):
    n, piece = acc.shape
    out_shape = [out((n, piece), bf16)]
    if part < PARTS - 1:
        stats = []
        out_shape += [out((n, 128), f32)]
    else:
        out_shape += [out((8, n), f32)] * 3
    return pl.pallas_call(
        functools.partial(last_kernel, part, len(stats), tile),
        grid_spec=pltpu.PrefetchScalarGridSpec(
            num_scalar_prefetch=1,
            grid=(1,),
            in_specs=[WHOLE] * (5 + len(stats)),
            out_specs=[WHOLE] * len(out_shape),
        ),
        out_shape=out_shape,
        compiler_params=params(10),
        cost_estimate=cost(2 * n * w.shape[0] * piece, 8 * n * piece, n * piece),
        name="last_draft",
    )(at, near(w), near(acc), near(hid), near(e_t), near(t_stat), *map(near, stats))


def hidden_kernel(nz, count, z_ref, *refs):
    slope_refs, w_refs = refs[:PARTS], refs[PARTS:PARTS + PARTS * count]
    out_ref, whole_ref, sem = refs[PARTS + PARTS * count:]

    @pl.when(pl.program_id(0) == 0)
    def _():
        waits = [
            assemble(
                z_ref[0], nz, count, w_refs[p * count:(p + 1) * count], whole_ref.at[p], sem.at[p]
            )
            for p in range(PARTS)
        ]
        for wait in waits:
            wait()

    tile = out_ref.shape[0]
    at = pl.ds(pl.multiple_of(pl.program_id(0) * tile, tile), tile)
    acc = dot_nt(slope_refs[0][at, :], whole_ref[0])
    for p in range(1, PARTS):
        acc = acc + dot_nt(slope_refs[p][at, :], whole_ref[p])
    out_ref[...] = acc.astype(bf16)


def hidden_call(nz, z, slope, blocks, dh, tile):
    n, piece = slope[0].shape
    count = len(blocks[0])
    row = lambda i, s: (i, 0)
    return pl.pallas_call(
        functools.partial(hidden_kernel, nz, count),
        grid_spec=pltpu.PrefetchScalarGridSpec(
            num_scalar_prefetch=1,
            grid=(n // tile,),
            in_specs=[WHOLE] * PARTS
            + [pl.BlockSpec(memory_space=pl.ANY)] * (PARTS * count),
            out_specs=pl.BlockSpec((tile, dh), row),
            scratch_shapes=[
                pltpu.VMEM((PARTS, dh, piece), bf16),
                pltpu.SemaphoreType.DMA((PARTS, count)),
            ],
        ),
        out_shape=jax.ShapeDtypeStruct((n, dh), bf16),
        compiler_params=params(16),
        cost_estimate=cost(2 * n * dh * piece * PARTS, 8 * n * piece),
        name="hidden_grad",
    )(z, *map(near, slope), *[b for bs in blocks for b in bs])


def fold_rows(a, b):
    t_top = jnp.maximum(a[0:1], b[0:1])
    fa, fb = jnp.exp(a[0:1] - t_top), jnp.exp(b[0:1] - t_top)
    z_top = jnp.maximum(a[3:4], b[3:4])
    ga, gb = jnp.exp(a[3:4] - z_top), jnp.exp(b[3:4] - z_top)
    rows = [
        t_top,
        a[1:2] * fa + b[1:2] * fb,
        a[2:3] * fa + b[2:3] * fb,
        z_top,
        a[4:5] * ga + b[4:5] * gb,
        a[5:6] + b[5:6],
    ]
    return jnp.concatenate(rows + [a[6:8]])


def fold_kernel(*refs):
    got = [r[...] for r in refs[:-1]]
    while len(got) > 1:
        got = [fold_rows(got[j], got[j + 1]) for j in range(0, len(got), 2)]
    refs[-1][...] = got[0]


def fold_call(rows):
    return pl.pallas_call(
        fold_kernel,
        in_specs=[WHOLE] * len(rows),
        out_specs=WHOLE,
        out_shape=out(rows[0].shape, f32),
        compiler_params=params(4),
        name="fold",
    )(*map(near, rows))


def slope_kernel(part, peers, idx_ref, *refs):
    step = pl.program_id(0)
    if peers:
        tops_ref = refs[peers]
        ez_ref, et_ref, ht_ref = refs[peers + 1:peers + 4]
        slope_ref, msg_ref, coef_ref, loss_ref = refs[peers + 4:]

        @pl.when(step == 0)
        def _():
            got = [r[...] for r in refs[:peers]]
            while len(got) > 1:
                got = [fold_rows(got[j], got[j + 1]) for j in range(0, len(got), 2)]
            s = got[0]
            t_inv = 1.0 / s[1:2]
            lse_t = s[0:1] + jnp.log(s[1:2])
            lse_z = s[3:4] + jnp.log(s[4:5])
            n = s.shape[1]
            per_token = s[2:3] * t_inv - lse_t + (1.0 + ce_weight) * lse_z - ce_weight * s[5:6]
            plane = jnp.sum(per_token[:, :n // 2], axis=1, keepdims=True) + jnp.sum(
                per_token[:, n // 2:], axis=1, keepdims=True
            )
            loss_ref[...] = jnp.broadcast_to(plane, loss_ref.shape)
            z_inv = (1.0 + ce_weight) / s[4:5]
            tops = tops_ref[...]
            rows = [jnp.exp(tops[0:1] - s[0:1]) * t_inv]
            rows += [jnp.exp(tops[p + 1:p + 2] - s[3:4]) * z_inv for p in range(PARTS)]
            rows += [tops[PARTS + 1:PARTS + 2]]
            rows += [jnp.zeros((128 - len(rows), n), f32)]
            coef_ref[...] = jnp.concatenate(rows).T

    else:
        coef_ref, ez_ref, et_ref, ht_ref, slope_ref, msg_ref = refs
    b = coef_ref[:, 0:1]
    a = coef_ref[:, part + 1:part + 2]
    piece = ez_ref.shape[1]
    tile = piece // pl.num_programs(0)
    first = pl.multiple_of(step * tile, tile)
    at = pl.ds(first, tile)
    e_t = et_ref[:, pl.ds(pl.multiple_of(part * piece + first, tile), tile)]
    value = ez_ref[:, at].astype(f32) * a - e_t.astype(f32) * b
    column = lax.broadcasted_iota(jnp.int32, value.shape, 1)
    id_col = coef_ref[:, PARTS + 1:PARTS + 2].astype(jnp.int32) - (part * piece + first)
    value = jnp.where(column == id_col, value - ce_weight, value)
    slope = value.astype(bf16)
    slope_ref[:, at] = slope
    deep = msg_ref.shape[0]
    rows = pl.ds(pl.multiple_of(idx_ref[0] * deep, deep), deep)
    msg_ref[...] = dot(ht_ref[rows, :], slope).astype(bf16)


def slope_call(part, index, head_args, e_z, e_t, hid_t, deep, tile):
    n, piece = e_z.shape
    peers = len(head_args) - 1
    out_specs = [WHOLE, pl.BlockSpec((deep, tile), lambda i, s: (0, i))]
    out_shape = [out((n, piece), bf16), jax.ShapeDtypeStruct((deep, piece), bf16)]
    if peers:
        out_specs += [WHOLE, WHOLE]
        out_shape += [out((n, 128), f32), out((8, 128), f32)]
    args = [*head_args, e_z, e_t, hid_t]
    return pl.pallas_call(
        functools.partial(slope_kernel, part, peers),
        grid_spec=pltpu.PrefetchScalarGridSpec(
            num_scalar_prefetch=1,
            grid=(piece // tile,),
            in_specs=[WHOLE] * len(args),
            out_specs=out_specs,
        ),
        out_shape=out_shape,
        compiler_params=params(16),
        cost_estimate=cost(2 * n * deep * piece, 6 * n * piece),
        name="slope",
    )(index, *map(near, args))


def loss_kernel(scale, z_ref, *refs):
    planes, out_ref = [r[...] for r in refs[:-1]], refs[-1]
    nz = len(planes)
    total = jnp.zeros(out_ref.shape, f32)
    for chip in range(nz):
        k = lax.rem(z_ref[0] - chip + nz, nz)
        term = planes[0]
        for j in range(1, nz):
            term = jnp.where(k == j, planes[j], term)
        total = total + term
    out_ref[...] = total * scale


def loss_call(z, planes, scale):
    return pl.pallas_call(
        functools.partial(loss_kernel, scale),
        grid_spec=pltpu.PrefetchScalarGridSpec(
            num_scalar_prefetch=1,
            grid=(1,),
            in_specs=[WHOLE] * len(planes),
            out_specs=WHOLE,
        ),
        out_shape=jax.ShapeDtypeStruct(planes[0].shape, f32),
        compiler_params=params(4),
        name="loss_sum",
    )(z, *planes)


def body(n_tok, n_voc, hidden, head, logits, ids):
    nz = n_tok // 2
    rows, dh = hidden.shape
    own_rows, share = head.shape
    half = share // 2
    piece = half // PARTS
    deep = 2 * own_rows
    tile = min(256, rows)
    wide = min(512, piece)
    me = lax.axis_index("tok")
    core = lax.rem(me, 2)
    z = lax.div(me, 2)
    voc = lax.axis_index("voc")
    width = dh // n_voc

    def here(kind, s):
        return z + jnp.where((lax.rem(z, 2) == 0) == (kind == "even"), s, -s)

    def inside(block):
        return jnp.logical_and(block >= 0, block < nz)

    def single(s):
        return not set(holders("even", nz, s)) & set(holders("odd", nz, s))

    def scalar(x):
        return jnp.reshape(x, (1,)).astype(jnp.int32)

    even = core == 0
    first_chip = z == 0
    row_of = {("own", 0): z}
    for s in range(1, nz):
        even_block, odd_block = here("even", s), here("odd", s)
        row_of["even", s] = jnp.clip(even_block, 0, nz - 1)
        row_of["odd", s] = jnp.clip(odd_block, 0, nz - 1)
        if single(s):
            either = jnp.where(inside(even_block), even_block, odd_block)
            row_of["even", s] = row_of["odd", s] = jnp.clip(either, 0, nz - 1)
    ahead = {
        "core": scalar(core),
        "z": scalar(z),
        "last": scalar(jnp.where(z == 0, nz - 1, 0)),
        "first": scalar(row_of["even", nz - 1]),
    }
    row_of = {k: v * deep for k, v in row_of.items()}
    col_of = [(voc ^ v) * width for v in range(n_voc)]
    vocab_start = voc * share + core * half
    (even, first_chip, ahead, row_of, col_of, vocab_start), head, hidden, logits, ids = (
        lax.optimization_barrier(
            ((even, first_chip, ahead, row_of, col_of, vocab_start), head, hidden, logits, ids)
        )
    )

    def swap(x):
        return lax.ppermute(x, "tok", [(i, i ^ 1) for i in range(n_tok)])

    def hop(x, pairs):
        return lax.ppermute(
            x, "tok", [(2 * a + k, 2 * b + k) for a, b in pairs for k in range(2)]
        )

    def plane_swap(x, v):
        return lax.ppermute(x, "voc", [(w, w ^ v) for w in range(n_voc)])

    def mine(x, other=False):
        left, right = x[:, :half], x[:, half:]
        return jnp.where(even, right, left) if other else jnp.where(even, left, right)

    keep, send = mine(head), mine(head, True)
    blocks = []
    for p in range(PARTS):
        cut = slice(p * piece, (p + 1) * piece)
        other = swap(send[:, cut])
        blocks.append(
            jnp.where(
                even,
                jnp.concatenate([keep[:, cut], other]),
                jnp.concatenate([other, keep[:, cut]]),
            )
        )

    came = [{("own", 0): b, ("even", 0): b, ("odd", 0): b} for b in blocks]
    other_kind = {"even": "odd", "odd": "even"}
    for s in range(1, nz):
        for p in range(PARTS):
            for kind in ("even", "odd"):
                pairs = [(edge(kind, a), a) for a in holders(kind, nz, s)]
                if pairs:
                    came[p][kind, s] = hop(came[p][other_kind[kind], s - 1], pairs)

    hid = jnp.concatenate([hidden, swap(hidden)])
    hid_t = turn_call(hid, tile)
    tgt = mine(logits, True)
    tgt = swap(tgt)
    local = jnp.concatenate([ids, swap(ids)]) - vocab_start
    e_t, t_stat = target_call(ahead["core"], logits, tgt, local[:, None], tile)

    stats, e_z = [], []
    order = arrivals(nz)
    whole = [[came[p][k] for k in order] for p in range(PARTS)]
    early = [k for k in order if k[1] < nz - 1]
    for p in range(PARTS):
        acc = early_call(nz, ahead["z"], whole[p][:len(early)], hid, tile)
        w = whole[p][len(early):]
        w = w[0] if len(w) == 1 else jnp.where(first_chip, w[0], w[1])
        outs = last_call(p, ahead["last"], w, acc, hid, e_t, t_stat, stats, tile)
        e_z.append(outs[0])
        if p < PARTS - 1:
            stats.append(outs[1])
    mine_rows, turned, tops = outs[1:]

    x = fold_call([mine_rows, swap(turned)])
    bits = n_voc.bit_length() - 1
    done = 0
    while True:
        few = min(1, bits - done)
        got = [x] + [plane_swap(x, v << done) for v in range(1, 1 << few)]
        done += few
        if done >= bits:
            break
        x = fold_call(got)

    msgs, slope = [], []
    for p in range(PARTS):
        head_args = got + [tops] if p == 0 else [coef]
        outs = slope_call(p, ahead["first"], head_args, e_z[p], e_t, hid_t, deep, wide)
        slope.append(outs[0])
        msgs.append(outs[1])
        if p == 0:
            coef, plane = outs[2:]

    def cut(x, row, col, shape):
        row, col = (jnp.asarray(i, jnp.int32) for i in (row, col))
        return lax.dynamic_slice(x, (row, col), shape, allow_negative_indices=False)

    def grad_rows(way, s, p):
        return dot(cut(hid_t, row_of[way, s], 0, (deep, 2 * rows)), slope[p])

    def add(x, *terms):
        for t in terms:
            if t is not None:
                x = x + t.astype(f32)
        return x

    got = [{} for _ in range(PARTS)]
    for s in range(nz - 1, 0, -1):
        for p in range(PARTS):
            for kind in ("even", "odd"):
                pairs = [(a, edge(kind, a)) for a in holders(kind, nz, s)]
                if not pairs:
                    continue
                back = {k: got[p].get((k, s + 1)) for k in other_kind}
                if s == nz - 1 and kind == "even":
                    msg = msgs[p]
                elif not single(s):
                    msg = add(grad_rows(kind, s, p), back[other_kind[kind]]).astype(bf16)
                elif kind == "even" or s == nz - 1:
                    msg = add(grad_rows(kind, s, p), *back.values()).astype(bf16)
                got[p][kind, s] = hop(msg, pairs)
    keeps, gives = [], []
    for p in range(PARTS):
        full = add(grad_rows("own", 0, p), got[p].get(("even", 1)), got[p].get(("odd", 1)))
        low, high = full[:own_rows], full[own_rows:]
        keeps.append(jnp.where(even, low, high))
        give = jnp.where(even, high, low).astype(bf16)
        gives.append(swap(give).astype(f32))
    grad_head = jnp.where(
        even,
        jnp.concatenate(keeps + gives, axis=1),
        jnp.concatenate(gives + keeps, axis=1),
    )

    late, plane, _ = lax.optimization_barrier((slope, plane, msgs[-1]))
    planes = [hop(plane, [(a, (a + k) % nz) for a in range(nz)]) for k in range(1, nz)]
    loss = loss_call(ahead["z"], [plane] + planes, 1.0 / (rows * n_tok))[0, 0]

    part = hidden_call(nz, ahead["z"], late, whole, dh, tile)
    part = part[:rows].astype(f32) + swap(part[rows:]).astype(f32)

    def wide_slice(v):
        return cut(part, 0, col_of[v], (rows, width))

    grad_hidden = wide_slice(0)
    for v in range(1, n_voc):
        came = plane_swap(wide_slice(v).astype(bf16), v)
        grad_hidden = grad_hidden + came.astype(f32)
    return loss, grad_hidden, grad_head


def solution(mesh):
    placed = (P("tok", None), P("tok", "voc"), P("tok", "voc"), P("tok"))
    n_tok, n_voc = mesh.shape["tok"], mesh.shape["voc"]
    return jax.shard_map(
        functools.partial(body, n_tok, n_voc),
        mesh=mesh,
        in_specs=placed,
        out_specs=(P(), P("tok", "voc"), P("tok", "voc")),
        check_vma=False,
    )
```

```python
import functools
import jax
import jax.numpy as jnp
from jax import lax
from jax.experimental import pallas as pl
from jax.experimental.pallas import tpu as pltpu
from jax.sharding import PartitionSpec as P


ce_weight = 0.5
PARTS = 2
f32, bf16 = jnp.float32, jnp.bfloat16


def dot(a, b):
    return lax.dot_general(a, b, (((1,), (0,)), ((), ())), preferred_element_type=f32)


def dot_nt(a, b):
    return lax.dot_general(a, b, (((1,), (1,)), ((), ())), preferred_element_type=f32)


def lanes(columns, like, first=0):
    lane = lax.broadcasted_iota(jnp.int32, like, 1)
    out = jnp.zeros(like, f32)
    for k, c in enumerate(columns):
        out = jnp.where(lane == first + k, c, out)
    return out


def block_of(kind, z, s):
    ahead = (z % 2 == 0) == (kind == "even")
    return z + s if ahead else z - s


def edge(kind, z):
    return z ^ 1 if kind == "even" else ((z + 1) ^ 1) - 1


def holders(kind, nz, s):
    return [z for z in range(nz) if 0 <= block_of(kind, z, s) < nz]


def arrivals(nz):
    return [("own", 0)] + [
        (kind, s) for s in range(1, nz) for kind in ("even", "odd") if holders(kind, nz, s)
    ]


def cost(flops, size, trans=0):
    return pl.CostEstimate(flops=flops, bytes_accessed=size, transcendentals=trans)


WHOLE = pl.BlockSpec(memory_space=pltpu.VMEM)


def near(x):
    return pltpu.with_memory_space_constraint(x, pltpu.VMEM)


def out(shape, dtype):
    return pltpu.VMEM(shape, dtype)


def params(size):
    return pltpu.CompilerParams(vmem_limit_bytes=size << 20)


def target_kernel(own_tiles, core_ref, mine_ref, came_ref, id_ref, e_ref, stat_ref):
    step = pl.program_id(0)
    t = jnp.where(step < own_tiles, mine_ref[...], came_ref[...]).astype(f32)
    at = pl.ds(pl.multiple_of(step * t.shape[0], t.shape[0]), t.shape[0])
    top = jnp.max(t, axis=1, keepdims=True)
    e = jnp.exp(t - top)
    e_ref[at, :] = e.astype(bf16)
    total = jnp.sum(e, axis=1, keepdims=True)
    first = jnp.sum(e * t, axis=1, keepdims=True)
    ids = id_ref[...].astype(f32)
    stat_ref[at, :] = lanes([top, total, first, ids], (t.shape[0], 128))


def target_call(core, logits, came, ids, tile):
    rows, half = came.shape
    n, own_tiles = 2 * rows, rows // tile
    return pl.pallas_call(
        functools.partial(target_kernel, own_tiles),
        grid_spec=pltpu.PrefetchScalarGridSpec(
            num_scalar_prefetch=1,
            grid=(n // tile,),
            in_specs=[
                pl.BlockSpec((tile, half), lambda i, s: (jnp.minimum(i, own_tiles - 1), s[0])),
                pl.BlockSpec((tile, half), lambda i, s: (jnp.maximum(i - own_tiles, 0), 0)),
                pl.BlockSpec((tile, 1), lambda i, s: (i, 0)),
            ],
            out_specs=[WHOLE, WHOLE],
        ),
        out_shape=[out((n, half), bf16), out((n, 128), f32)],
        compiler_params=params(16),
        cost_estimate=cost(8 * n * half, 4 * n * half, n * half),
        name="target_exps",
    )(core, logits, came, ids)


def turn_kernel(tile, x_ref, out_ref):
    for k in range(x_ref.shape[0] // tile):
        at = slice(k * tile, (k + 1) * tile)
        out_ref[:, at] = x_ref[at, :].T


def turn_call(x, tile):
    n, dh = x.shape
    return pl.pallas_call(
        functools.partial(turn_kernel, tile),
        in_specs=[WHOLE],
        out_specs=WHOLE,
        out_shape=out((dh, n), bf16),
        compiler_params=params(8),
        cost_estimate=cost(0, 4 * n * dh),
        name="turn",
    )(near(x))


def assemble(z, nz, count, refs, whole_ref, sem):
    deep = refs[0].shape[0]
    given = arrivals(nz)[:count]

    def place(block):
        return pl.ds(pl.multiple_of(block * deep, deep), deep)

    def each(act):
        for k, (kind, s) in enumerate(given):
            if kind == "own":
                act(k, z)
                continue
            sign = jnp.where((lax.rem(z, 2) == 0) == (kind == "even"), 1, -1)
            block = z + sign * s

            @pl.when(jnp.logical_and(block >= 0, block < nz))
            def _(k=k, block=block):
                act(k, block)

    def copy(k, block):
        return pltpu.make_async_copy(refs[k], whole_ref.at[place(block), :], sem.at[k])

    each(lambda k, block: copy(k, block).start())
    if count < len(arrivals(nz)):

        @pl.when(jnp.logical_or(z == 0, z == nz - 1))
        def _():
            hole = jnp.where(z == 0, nz - 1, 0)
            whole_ref[place(hole), :] = jnp.zeros((deep, whole_ref.shape[1]), bf16)

    return lambda: each(lambda k, block: copy(k, block).wait())


def early_kernel(nz, count, z_ref, *refs):
    w_refs = refs[:count]
    h_ref, acc_ref, whole_ref, sem = refs[count:]

    @pl.when(pl.program_id(0) == 0)
    def _():
        assemble(z_ref[0], nz, count, w_refs, whole_ref, sem)()

    tile = h_ref.shape[0] // pl.num_programs(0)
    at = pl.ds(pl.multiple_of(pl.program_id(0) * tile, tile), tile)
    acc_ref[at, :] = dot(h_ref[at, :], whole_ref[...])


def early_call(nz, z, blocks, hid, tile):
    n, dh = hid.shape
    piece = blocks[0].shape[1]
    return pl.pallas_call(
        functools.partial(early_kernel, nz, len(blocks)),
        grid_spec=pltpu.PrefetchScalarGridSpec(
            num_scalar_prefetch=1,
            grid=(n // tile,),
            in_specs=[pl.BlockSpec(memory_space=pl.ANY)] * len(blocks) + [WHOLE],
            out_specs=WHOLE,
            scratch_shapes=[
                pltpu.VMEM((dh, piece), bf16),
                pltpu.SemaphoreType.DMA((len(blocks),)),
            ],
        ),
        out_shape=out((n, piece), f32),
        compiler_params=params(10),
        cost_estimate=cost(2 * n * dh * piece, 6 * n * piece),
        name="early_draft",
    )(z, *blocks, near(hid))


def last_kernel(part, earlier, tile, at_ref, *refs):
    w_ref, acc_ref, h_ref, e_ref, t_ref = refs[:5]
    stat_refs = refs[5:5 + earlier]
    outs = refs[5 + earlier:]
    n, piece = acc_ref.shape
    deep = w_ref.shape[0]
    block = pl.ds(pl.multiple_of(at_ref[0] * deep, deep), deep)
    like = (tile, 128)
    for k in range(n // tile):
        at = slice(k * tile, (k + 1) * tile)
        z = acc_ref[at, :] + dot(h_ref[at, block], w_ref[...])
        top = jnp.max(z, axis=1, keepdims=True)
        e = jnp.exp(z - top)
        outs[0][at, :] = e.astype(bf16)
        total = jnp.sum(e, axis=1, keepdims=True)
        e_t = e_ref[at, part * piece:(part + 1) * piece].astype(f32)
        cross = jnp.sum(e_t * z, axis=1, keepdims=True)
        t_stat = t_ref[at, :]
        column = lax.broadcasted_iota(jnp.int32, z.shape, 1) + part * piece
        id_col = t_stat[:, 3:4].astype(jnp.int32)
        own = jnp.sum(jnp.where(column == id_col, z, 0.0), axis=1, keepdims=True)
        stat = lanes([top, total, cross, own], like, 4 + 4 * part)
        if part < PARTS - 1:
            outs[1][at, :] = stat
            continue
        send_ref, turn_ref, tops_ref = outs[1:]
        stat = stat + t_stat
        for r in stat_refs:
            stat = stat + r[at, :]
        row = stat.T
        row = [row[k:k + 1] for k in range(4 + 4 * PARTS)]
        tops = row[4::4]
        all_top = functools.reduce(jnp.maximum, tops)
        total = sum(row[5 + 4 * p] * jnp.exp(tops[p] - all_top) for p in range(PARTS))
        cross, own = sum(row[6::4]), sum(row[7::4])
        blank = jnp.zeros((1, tile), f32)
        rows = [row[0], row[1], row[2] - cross, all_top, total, own, blank, blank]
        rows = jnp.concatenate(rows)
        send_ref[:, at] = rows
        turned = (k * tile + n // 2) % n
        turn_ref[:, turned:turned + tile] = rows
        tops = [row[0]] + tops + [row[3]]
        tops_ref[:, at] = jnp.concatenate(tops + [blank] * (8 - len(tops)))


def last_call(part, at, w, acc, hid, e_t, t_stat, stats, tile):
    n, piece = acc.shape
    out_shape = [out((n, piece), bf16)]
    if part < PARTS - 1:
        stats = []
        out_shape += [out((n, 128), f32)]
    else:
        out_shape += [out((8, n), f32)] * 3
    return pl.pallas_call(
        functools.partial(last_kernel, part, len(stats), tile),
        grid_spec=pltpu.PrefetchScalarGridSpec(
            num_scalar_prefetch=1,
            grid=(1,),
            in_specs=[WHOLE] * (5 + len(stats)),
            out_specs=[WHOLE] * len(out_shape),
        ),
        out_shape=out_shape,
        compiler_params=params(10),
        cost_estimate=cost(2 * n * w.shape[0] * piece, 8 * n * piece, n * piece),
        name="last_draft",
    )(at, near(w), near(acc), near(hid), near(e_t), near(t_stat), *map(near, stats))


def hidden_kernel(nz, count, z_ref, *refs):
    slope_refs, w_refs = refs[:PARTS], refs[PARTS:PARTS + PARTS * count]
    out_ref, whole_ref, sem = refs[PARTS + PARTS * count:]

    @pl.when(pl.program_id(0) == 0)
    def _():
        waits = [
            assemble(
                z_ref[0], nz, count, w_refs[p * count:(p + 1) * count], whole_ref.at[p], sem.at[p]
            )
            for p in range(PARTS)
        ]
        for wait in waits:
            wait()

    tile = out_ref.shape[0]
    at = pl.ds(pl.multiple_of(pl.program_id(0) * tile, tile), tile)
    acc = dot_nt(slope_refs[0][at, :], whole_ref[0])
    for p in range(1, PARTS):
        acc = acc + dot_nt(slope_refs[p][at, :], whole_ref[p])
    out_ref[...] = acc.astype(bf16)


def hidden_call(nz, z, slope, blocks, dh, tile):
    n, piece = slope[0].shape
    count = len(blocks[0])
    row = lambda i, s: (i, 0)
    return pl.pallas_call(
        functools.partial(hidden_kernel, nz, count),
        grid_spec=pltpu.PrefetchScalarGridSpec(
            num_scalar_prefetch=1,
            grid=(n // tile,),
            in_specs=[WHOLE] * PARTS
            + [pl.BlockSpec(memory_space=pl.ANY)] * (PARTS * count),
            out_specs=pl.BlockSpec((tile, dh), row),
            scratch_shapes=[
                pltpu.VMEM((PARTS, dh, piece), bf16),
                pltpu.SemaphoreType.DMA((PARTS, count)),
            ],
        ),
        out_shape=jax.ShapeDtypeStruct((n, dh), bf16),
        compiler_params=params(16),
        cost_estimate=cost(2 * n * dh * piece * PARTS, 8 * n * piece),
        name="hidden_grad",
    )(z, *map(near, slope), *[b for bs in blocks for b in bs])


def fold_rows(a, b):
    t_top = jnp.maximum(a[0:1], b[0:1])
    fa, fb = jnp.exp(a[0:1] - t_top), jnp.exp(b[0:1] - t_top)
    z_top = jnp.maximum(a[3:4], b[3:4])
    ga, gb = jnp.exp(a[3:4] - z_top), jnp.exp(b[3:4] - z_top)
    rows = [
        t_top,
        a[1:2] * fa + b[1:2] * fb,
        a[2:3] * fa + b[2:3] * fb,
        z_top,
        a[4:5] * ga + b[4:5] * gb,
        a[5:6] + b[5:6],
    ]
    return jnp.concatenate(rows + [a[6:8]])


def fold_kernel(*refs):
    got = [r[...] for r in refs[:-1]]
    while len(got) > 1:
        got = [fold_rows(got[j], got[j + 1]) for j in range(0, len(got), 2)]
    refs[-1][...] = got[0]


def fold_call(rows):
    return pl.pallas_call(
        fold_kernel,
        in_specs=[WHOLE] * len(rows),
        out_specs=WHOLE,
        out_shape=out(rows[0].shape, f32),
        compiler_params=params(4),
        name="fold",
    )(*map(near, rows))


def slope_kernel(part, peers, tile, idx_ref, *refs):
    if peers:
        tops_ref = refs[peers]
        ez_ref, et_ref, ht_ref = refs[peers + 1:peers + 4]
        slope_ref, msg_ref, coef_ref, loss_ref = refs[peers + 4:]

        got = [r[...] for r in refs[:peers]]
        while len(got) > 1:
            got = [fold_rows(got[j], got[j + 1]) for j in range(0, len(got), 2)]
        s = got[0]
        t_inv = 1.0 / s[1:2]
        lse_t = s[0:1] + jnp.log(s[1:2])
        lse_z = s[3:4] + jnp.log(s[4:5])
        n = s.shape[1]
        per_token = s[2:3] * t_inv - lse_t + (1.0 + ce_weight) * lse_z - ce_weight * s[5:6]
        plane = jnp.sum(per_token[:, :n // 2], axis=1, keepdims=True) + jnp.sum(
            per_token[:, n // 2:], axis=1, keepdims=True
        )
        loss_ref[...] = jnp.broadcast_to(plane, loss_ref.shape)
        z_inv = (1.0 + ce_weight) / s[4:5]
        tops = tops_ref[...]
        rows = [jnp.exp(tops[0:1] - s[0:1]) * t_inv]
        rows += [jnp.exp(tops[p + 1:p + 2] - s[3:4]) * z_inv for p in range(PARTS)]
        rows += [tops[PARTS + 1:PARTS + 2]]
        rows += [jnp.zeros((128 - len(rows), n), f32)]
        coef_ref[...] = jnp.concatenate(rows).T

    else:
        coef_ref, ez_ref, et_ref, ht_ref, slope_ref, msg_ref = refs
    b = coef_ref[:, 0:1]
    a = coef_ref[:, part + 1:part + 2]
    id_col = coef_ref[:, PARTS + 1:PARTS + 2].astype(jnp.int32)
    deep, piece = msg_ref.shape
    rows = pl.ds(pl.multiple_of(idx_ref[0] * deep, deep), deep)
    for first in range(0, piece, tile):
        at = slice(first, first + tile)
        e_t = et_ref[:, part * piece + first:part * piece + first + tile]
        value = ez_ref[:, at].astype(f32) * a - e_t.astype(f32) * b
        column = lax.broadcasted_iota(jnp.int32, value.shape, 1) + (part * piece + first)
        value = jnp.where(column == id_col, value - ce_weight, value)
        slope = value.astype(bf16)
        slope_ref[:, at] = slope
        msg_ref[:, at] = dot(ht_ref[rows, :], slope).astype(bf16)


def slope_call(part, index, head_args, e_z, e_t, hid_t, deep, tile):
    n, piece = e_z.shape
    peers = len(head_args) - 1
    out_specs = [WHOLE, WHOLE]
    out_shape = [out((n, piece), bf16), out((deep, piece), bf16)]
    if peers:
        out_specs += [WHOLE, WHOLE]
        out_shape += [out((n, 128), f32), out((8, 128), f32)]
    args = [*head_args, e_z, e_t, hid_t]
    return pl.pallas_call(
        functools.partial(slope_kernel, part, peers, tile),
        grid_spec=pltpu.PrefetchScalarGridSpec(
            num_scalar_prefetch=1,
            grid=(1,),
            in_specs=[WHOLE] * len(args),
            out_specs=out_specs,
        ),
        out_shape=out_shape,
        compiler_params=params(16),
        cost_estimate=cost(2 * n * deep * piece, 6 * n * piece),
        name="slope",
    )(index, *map(near, args))


def loss_kernel(scale, z_ref, *refs):
    planes, out_ref = [r[...] for r in refs[:-1]], refs[-1]
    nz = len(planes)
    total = jnp.zeros(out_ref.shape, f32)
    for chip in range(nz):
        k = lax.rem(z_ref[0] - chip + nz, nz)
        term = planes[0]
        for j in range(1, nz):
            term = jnp.where(k == j, planes[j], term)
        total = total + term
    out_ref[...] = total * scale


def loss_call(z, planes, scale):
    return pl.pallas_call(
        functools.partial(loss_kernel, scale),
        grid_spec=pltpu.PrefetchScalarGridSpec(
            num_scalar_prefetch=1,
            grid=(1,),
            in_specs=[WHOLE] * len(planes),
            out_specs=WHOLE,
        ),
        out_shape=jax.ShapeDtypeStruct(planes[0].shape, f32),
        compiler_params=params(4),
        name="loss_sum",
    )(z, *planes)


def body(n_tok, n_voc, hidden, head, logits, ids):
    nz = n_tok // 2
    rows, dh = hidden.shape
    own_rows, share = head.shape
    half = share // 2
    piece = half // PARTS
    deep = 2 * own_rows
    tile = min(256, rows)
    wide = min(256, piece)
    me = lax.axis_index("tok")
    core = lax.rem(me, 2)
    z = lax.div(me, 2)
    voc = lax.axis_index("voc")
    width = dh // n_voc

    def here(kind, s):
        return z + jnp.where((lax.rem(z, 2) == 0) == (kind == "even"), s, -s)

    def inside(block):
        return jnp.logical_and(block >= 0, block < nz)

    def single(s):
        return not set(holders("even", nz, s)) & set(holders("odd", nz, s))

    def scalar(x):
        return jnp.reshape(x, (1,)).astype(jnp.int32)

    even = core == 0
    first_chip = z == 0
    row_of = {("own", 0): z}
    for s in range(1, nz):
        even_block, odd_block = here("even", s), here("odd", s)
        row_of["even", s] = jnp.clip(even_block, 0, nz - 1)
        row_of["odd", s] = jnp.clip(odd_block, 0, nz - 1)
        if single(s):
            either = jnp.where(inside(even_block), even_block, odd_block)
            row_of["even", s] = row_of["odd", s] = jnp.clip(either, 0, nz - 1)
    ahead = {
        "core": scalar(core),
        "z": scalar(z),
        "last": scalar(jnp.where(z == 0, nz - 1, 0)),
        "first": scalar(row_of["even", nz - 1]),
    }
    row_of = {k: v * deep for k, v in row_of.items()}
    col_of = [(voc ^ v) * width for v in range(n_voc)]
    vocab_start = voc * share + core * half
    keep_cols = [core * half + p * piece for p in range(PARTS)]
    send_cols = [(1 - core) * half + p * piece for p in range(PARTS)]
    (even, first_chip, ahead, row_of, col_of, vocab_start, keep_cols, send_cols), head, hidden, logits, ids = (
        lax.optimization_barrier(
            ((even, first_chip, ahead, row_of, col_of, vocab_start, keep_cols, send_cols), head, hidden, logits, ids)
        )
    )

    def swap(x):
        return lax.ppermute(x, "tok", [(i, i ^ 1) for i in range(n_tok)])

    def hop(x, pairs):
        return lax.ppermute(x, "tok", [(2 * a + k, 2 * b + k) for a, b in pairs for k in range(2)])

    def plane_swap(x, v):
        return lax.ppermute(x, "voc", [(w, w ^ v) for w in range(n_voc)])

    def cut(x, row, col, shape):
        row, col = (jnp.asarray(i, jnp.int32) for i in (row, col))
        return lax.dynamic_slice(x, (row, col), shape, allow_negative_indices=False)

    def mine(x, other=False):
        left, right = x[:, :half], x[:, half:]
        return jnp.where(even, right, left) if other else jnp.where(even, left, right)

    blocks = []
    for p in range(PARTS):
        keep, send = (cut(head, 0, c[p], (own_rows, piece)) for c in (keep_cols, send_cols))
        other = swap(send)
        blocks.append(
            jnp.where(even, jnp.concatenate([keep, other]), jnp.concatenate([other, keep]))
        )

    came = [{("own", 0): b, ("even", 0): b, ("odd", 0): b} for b in blocks]
    other_kind = {"even": "odd", "odd": "even"}
    for s in range(1, nz):
        for p in range(PARTS):
            for kind in ("even", "odd"):
                pairs = [(edge(kind, a), a) for a in holders(kind, nz, s)]
                if pairs:
                    came[p][kind, s] = hop(came[p][other_kind[kind], s - 1], pairs)

    hid = jnp.concatenate([hidden, swap(hidden)])
    hid_t = turn_call(hid, tile)
    tgt = mine(logits, True)
    tgt = swap(tgt)
    local = jnp.concatenate([ids, swap(ids)]) - vocab_start
    e_t, t_stat = target_call(ahead["core"], logits, tgt, local[:, None], tile)

    stats, e_z = [], []
    order = arrivals(nz)
    whole = [[came[p][k] for k in order] for p in range(PARTS)]
    early = [k for k in order if k[1] < nz - 1]
    for p in range(PARTS):
        acc = early_call(nz, ahead["z"], whole[p][:len(early)], hid, tile)
        w = whole[p][len(early):]
        w = w[0] if len(w) == 1 else jnp.where(first_chip, w[0], w[1])
        outs = last_call(p, ahead["last"], w, acc, hid, e_t, t_stat, stats, tile)
        e_z.append(outs[0])
        if p < PARTS - 1:
            stats.append(outs[1])
    mine_rows, turned, tops = outs[1:]

    x = fold_call([mine_rows, swap(turned)])
    bits = n_voc.bit_length() - 1
    done = 0
    while True:
        few = min(1, bits - done)
        got = [x] + [plane_swap(x, v << done) for v in range(1, 1 << few)]
        done += few
        if done >= bits:
            break
        x = fold_call(got)

    msgs, slope = [], []
    for p in range(PARTS):
        head_args = got + [tops] if p == 0 else [coef]
        outs = slope_call(
            p, ahead["first"], head_args, e_z[p], e_t, hid_t, deep, wide
        )
        slope.append(outs[0])
        msgs.append(outs[1])
        if p == 0:
            coef, plane = outs[2:]

    def grad_rows(way, s, p):
        return dot(cut(hid_t, row_of[way, s], 0, (deep, 2 * rows)), slope[p])

    def add(x, *terms):
        for t in terms:
            if t is not None:
                x = x + t.astype(f32)
        return x

    got = [{} for _ in range(PARTS)]
    for s in range(nz - 1, 0, -1):
        for p in range(PARTS):
            for kind in ("even", "odd"):
                pairs = [(a, edge(kind, a)) for a in holders(kind, nz, s)]
                if not pairs:
                    continue
                back = {k: got[p].get((k, s + 1)) for k in other_kind}
                if s == nz - 1 and kind == "even":
                    msg = msgs[p]
                elif not single(s):
                    msg = add(grad_rows(kind, s, p), back[other_kind[kind]]).astype(bf16)
                elif kind == "even" or s == nz - 1:
                    msg = add(grad_rows(kind, s, p), *back.values()).astype(bf16)
                got[p][kind, s] = hop(msg, pairs)
    keeps, gives = [], []
    for p in range(PARTS):
        full = add(grad_rows("own", 0, p), got[p].get(("even", 1)), got[p].get(("odd", 1)))
        low, high = full[:own_rows], full[own_rows:]
        keeps.append(jnp.where(even, low, high))
        give = jnp.where(even, high, low).astype(bf16)
        gives.append(swap(give).astype(f32))
    grad_head = jnp.where(
        even,
        jnp.concatenate(keeps + gives, axis=1),
        jnp.concatenate(gives + keeps, axis=1),
    )

    late, plane, _ = lax.optimization_barrier((slope, plane, msgs[-1]))
    planes = [hop(plane, [(a, (a + k) % nz) for a in range(nz)]) for k in range(1, nz)]
    loss = loss_call(ahead["z"], [plane] + planes, 1.0 / (rows * n_tok))[0, 0]

    part = hidden_call(nz, ahead["z"], late, whole, dh, tile)
    part = part[:rows].astype(f32) + swap(part[rows:]).astype(f32)

    def wide_slice(v):
        return cut(part, 0, col_of[v], (rows, width))

    grad_hidden = wide_slice(0)
    for v in range(1, n_voc):
        came = plane_swap(wide_slice(v).astype(bf16), v)
        grad_hidden = grad_hidden + came.astype(f32)
    return loss, grad_hidden, grad_head


def solution(mesh):
    placed = (P("tok", None), P("tok", "voc"), P("tok", "voc"), P("tok"))
    n_tok, n_voc = mesh.shape["tok"], mesh.shape["voc"]
    return jax.shard_map(
        functools.partial(body, n_tok, n_voc),
        mesh=mesh,
        in_specs=placed,
        out_specs=(P(), P("tok", "voc"), P("tok", "voc")),
        check_vma=False,
    )
```

```python
import functools
import jax
import jax.numpy as jnp
from jax import lax
from jax.experimental import pallas as pl
from jax.experimental.pallas import tpu as pltpu
from jax.sharding import PartitionSpec as P


ce_weight = 0.5
PARTS = 2
f32, bf16 = jnp.float32, jnp.bfloat16


def dot(a, b):
    return lax.dot_general(a, b, (((1,), (0,)), ((), ())), preferred_element_type=f32)


def dot_nt(a, b):
    return lax.dot_general(a, b, (((1,), (1,)), ((), ())), preferred_element_type=f32)


def lanes(columns, like, first=0):
    lane = lax.broadcasted_iota(jnp.int32, like, 1)
    out = jnp.zeros(like, f32)
    for k, c in enumerate(columns):
        out = jnp.where(lane == first + k, c, out)
    return out


def block_of(kind, z, s):
    ahead = (z % 2 == 0) == (kind == "even")
    return z + s if ahead else z - s


def edge(kind, z):
    return z ^ 1 if kind == "even" else ((z + 1) ^ 1) - 1


def holders(kind, nz, s):
    return [z for z in range(nz) if 0 <= block_of(kind, z, s) < nz]


def arrivals(nz):
    return [("own", 0)] + [
        (kind, s) for s in range(1, nz) for kind in ("even", "odd") if holders(kind, nz, s)
    ]


def cost(flops, size, trans=0):
    return pl.CostEstimate(flops=flops, bytes_accessed=size, transcendentals=trans)


WHOLE = pl.BlockSpec(memory_space=pltpu.VMEM)


def near(x):
    return pltpu.with_memory_space_constraint(x, pltpu.VMEM)


def out(shape, dtype):
    return pltpu.VMEM(shape, dtype)


def params(size):
    return pltpu.CompilerParams(vmem_limit_bytes=size << 20)


def target_kernel(own_tiles, core_ref, mine_ref, came_ref, id_ref, e_ref, stat_ref):
    step = pl.program_id(0)
    t = jnp.where(step < own_tiles, mine_ref[...], came_ref[...]).astype(f32)
    at = pl.ds(pl.multiple_of(step * t.shape[0], t.shape[0]), t.shape[0])
    top = jnp.max(t, axis=1, keepdims=True)
    e = jnp.exp(t - top)
    e_ref[at, :] = e.astype(bf16)
    total = jnp.sum(e, axis=1, keepdims=True)
    first = jnp.sum(e * t, axis=1, keepdims=True)
    ids = id_ref[...].astype(f32)
    stat_ref[at, :] = lanes([top, total, first, ids], (t.shape[0], 128))


def target_call(core, logits, came, ids, tile):
    rows, half = came.shape
    n, own_tiles = 2 * rows, rows // tile
    return pl.pallas_call(
        functools.partial(target_kernel, own_tiles),
        grid_spec=pltpu.PrefetchScalarGridSpec(
            num_scalar_prefetch=1,
            grid=(n // tile,),
            in_specs=[
                pl.BlockSpec((tile, half), lambda i, s: (jnp.minimum(i, own_tiles - 1), s[0])),
                pl.BlockSpec((tile, half), lambda i, s: (jnp.maximum(i - own_tiles, 0), 0)),
                pl.BlockSpec((tile, 1), lambda i, s: (i, 0)),
            ],
            out_specs=[WHOLE, WHOLE],
        ),
        out_shape=[out((n, half), bf16), out((n, 128), f32)],
        compiler_params=params(16),
        cost_estimate=cost(8 * n * half, 4 * n * half, n * half),
        name="target_exps",
    )(core, logits, came, ids)


def turn_kernel(tile, x_ref, out_ref):
    for k in range(x_ref.shape[0] // tile):
        at = slice(k * tile, (k + 1) * tile)
        out_ref[:, at] = x_ref[at, :].T


def turn_call(x, tile):
    n, dh = x.shape
    return pl.pallas_call(
        functools.partial(turn_kernel, tile),
        in_specs=[WHOLE],
        out_specs=WHOLE,
        out_shape=out((dh, n), bf16),
        compiler_params=params(8),
        cost_estimate=cost(0, 4 * n * dh),
        name="turn",
    )(near(x))


def assemble(z, nz, count, refs, whole_ref, sem):
    deep = refs[0].shape[0]
    given = arrivals(nz)[:count]

    def place(block):
        return pl.ds(pl.multiple_of(block * deep, deep), deep)

    def each(act):
        for k, (kind, s) in enumerate(given):
            if kind == "own":
                act(k, z)
                continue
            sign = jnp.where((lax.rem(z, 2) == 0) == (kind == "even"), 1, -1)
            block = z + sign * s

            @pl.when(jnp.logical_and(block >= 0, block < nz))
            def _(k=k, block=block):
                act(k, block)

    def copy(k, block):
        return pltpu.make_async_copy(refs[k], whole_ref.at[place(block), :], sem.at[k])

    each(lambda k, block: copy(k, block).start())
    if count < len(arrivals(nz)):

        @pl.when(jnp.logical_or(z == 0, z == nz - 1))
        def _():
            hole = jnp.where(z == 0, nz - 1, 0)
            whole_ref[place(hole), :] = jnp.zeros((deep, whole_ref.shape[1]), bf16)

    return lambda: each(lambda k, block: copy(k, block).wait())


def early_kernel(nz, count, z_ref, *refs):
    w_refs = refs[:count]
    h_ref, acc_ref, whole_ref, sem = refs[count:]

    @pl.when(pl.program_id(0) == 0)
    def _():
        assemble(z_ref[0], nz, count, w_refs, whole_ref, sem)()

    tile = h_ref.shape[0] // pl.num_programs(0)
    at = pl.ds(pl.multiple_of(pl.program_id(0) * tile, tile), tile)
    acc_ref[at, :] = dot(h_ref[at, :], whole_ref[...])


def early_call(nz, z, blocks, hid, tile):
    n, dh = hid.shape
    piece = blocks[0].shape[1]
    return pl.pallas_call(
        functools.partial(early_kernel, nz, len(blocks)),
        grid_spec=pltpu.PrefetchScalarGridSpec(
            num_scalar_prefetch=1,
            grid=(n // tile,),
            in_specs=[pl.BlockSpec(memory_space=pl.ANY)] * len(blocks) + [WHOLE],
            out_specs=WHOLE,
            scratch_shapes=[
                pltpu.VMEM((dh, piece), bf16),
                pltpu.SemaphoreType.DMA((len(blocks),)),
            ],
        ),
        out_shape=out((n, piece), f32),
        compiler_params=params(10),
        cost_estimate=cost(2 * n * dh * piece, 6 * n * piece),
        name="early_draft",
    )(z, *blocks, near(hid))


def last_kernel(part, earlier, tile, at_ref, *refs):
    w_ref, acc_ref, h_ref, e_ref, t_ref = refs[:5]
    stat_refs = refs[5:5 + earlier]
    outs = refs[5 + earlier:]
    n, piece = acc_ref.shape
    deep = w_ref.shape[0]
    block = pl.ds(pl.multiple_of(at_ref[0] * deep, deep), deep)
    like = (tile, 128)
    for k in range(n // tile):
        at = slice(k * tile, (k + 1) * tile)
        z = acc_ref[at, :] + dot(h_ref[at, block], w_ref[...])
        top = jnp.max(z, axis=1, keepdims=True)
        e = jnp.exp(z - top)
        outs[0][at, :] = e.astype(bf16)
        total = jnp.sum(e, axis=1, keepdims=True)
        e_t = e_ref[at, part * piece:(part + 1) * piece].astype(f32)
        cross = jnp.sum(e_t * z, axis=1, keepdims=True)
        t_stat = t_ref[at, :]
        column = lax.broadcasted_iota(jnp.int32, z.shape, 1) + part * piece
        id_col = t_stat[:, 3:4].astype(jnp.int32)
        own = jnp.sum(jnp.where(column == id_col, z, 0.0), axis=1, keepdims=True)
        stat = lanes([top, total, cross, own], like, 4 + 4 * part)
        if part < PARTS - 1:
            outs[1][at, :] = stat
            continue
        send_ref, turn_ref, tops_ref = outs[1:]
        stat = stat + t_stat
        for r in stat_refs:
            stat = stat + r[at, :]
        row = stat.T
        row = [row[k:k + 1] for k in range(4 + 4 * PARTS)]
        tops = row[4::4]
        all_top = functools.reduce(jnp.maximum, tops)
        total = sum(row[5 + 4 * p] * jnp.exp(tops[p] - all_top) for p in range(PARTS))
        cross, own = sum(row[6::4]), sum(row[7::4])
        blank = jnp.zeros((1, tile), f32)
        rows = [row[0], row[1], row[2] - cross, all_top, total, own, blank, blank]
        rows = jnp.concatenate(rows)
        send_ref[:, at] = rows
        turned = (k * tile + n // 2) % n
        turn_ref[:, turned:turned + tile] = rows
        tops = [row[0]] + tops + [row[3]]
        tops_ref[:, at] = jnp.concatenate(tops + [blank] * (8 - len(tops)))


def last_call(part, at, w, acc, hid, e_t, t_stat, stats, tile):
    n, piece = acc.shape
    out_shape = [out((n, piece), bf16)]
    if part < PARTS - 1:
        stats = []
        out_shape += [out((n, 128), f32)]
    else:
        out_shape += [out((8, n), f32)] * 3
    return pl.pallas_call(
        functools.partial(last_kernel, part, len(stats), tile),
        grid_spec=pltpu.PrefetchScalarGridSpec(
            num_scalar_prefetch=1,
            grid=(1,),
            in_specs=[WHOLE] * (5 + len(stats)),
            out_specs=[WHOLE] * len(out_shape),
        ),
        out_shape=out_shape,
        compiler_params=params(10),
        cost_estimate=cost(2 * n * w.shape[0] * piece, 8 * n * piece, n * piece),
        name="last_draft",
    )(at, near(w), near(acc), near(hid), near(e_t), near(t_stat), *map(near, stats))


def hidden_kernel(nz, count, z_ref, *refs):
    slope_refs, w_refs = refs[:PARTS], refs[PARTS:PARTS + PARTS * count]
    out_ref, whole_ref, sem = refs[PARTS + PARTS * count:]

    @pl.when(pl.program_id(0) == 0)
    def _():
        waits = [
            assemble(
                z_ref[0], nz, count, w_refs[p * count:(p + 1) * count], whole_ref.at[p], sem.at[p]
            )
            for p in range(PARTS)
        ]
        for wait in waits:
            wait()

    tile = out_ref.shape[0]
    at = pl.ds(pl.multiple_of(pl.program_id(0) * tile, tile), tile)
    acc = dot_nt(slope_refs[0][at, :], whole_ref[0])
    for p in range(1, PARTS):
        acc = acc + dot_nt(slope_refs[p][at, :], whole_ref[p])
    out_ref[...] = acc.astype(bf16)


def hidden_call(nz, z, slope, blocks, dh, tile):
    n, piece = slope[0].shape
    count = len(blocks[0])
    row = lambda i, s: (i, 0)
    return pl.pallas_call(
        functools.partial(hidden_kernel, nz, count),
        grid_spec=pltpu.PrefetchScalarGridSpec(
            num_scalar_prefetch=1,
            grid=(n // tile,),
            in_specs=[WHOLE] * PARTS
            + [pl.BlockSpec(memory_space=pl.ANY)] * (PARTS * count),
            out_specs=pl.BlockSpec((tile, dh), row),
            scratch_shapes=[
                pltpu.VMEM((PARTS, dh, piece), bf16),
                pltpu.SemaphoreType.DMA((PARTS, count)),
            ],
        ),
        out_shape=jax.ShapeDtypeStruct((n, dh), bf16),
        compiler_params=params(16),
        cost_estimate=cost(2 * n * dh * piece * PARTS, 8 * n * piece),
        name="hidden_grad",
    )(z, *map(near, slope), *[b for bs in blocks for b in bs])


def fold_rows(a, b):
    t_top = jnp.maximum(a[0:1], b[0:1])
    fa, fb = jnp.exp(a[0:1] - t_top), jnp.exp(b[0:1] - t_top)
    z_top = jnp.maximum(a[3:4], b[3:4])
    ga, gb = jnp.exp(a[3:4] - z_top), jnp.exp(b[3:4] - z_top)
    rows = [
        t_top,
        a[1:2] * fa + b[1:2] * fb,
        a[2:3] * fa + b[2:3] * fb,
        z_top,
        a[4:5] * ga + b[4:5] * gb,
        a[5:6] + b[5:6],
    ]
    return jnp.concatenate(rows + [a[6:8]])


def fold_kernel(*refs):
    got = [r[...] for r in refs[:-1]]
    while len(got) > 1:
        got = [fold_rows(got[j], got[j + 1]) for j in range(0, len(got), 2)]
    refs[-1][...] = got[0]


def fold_call(rows):
    return pl.pallas_call(
        fold_kernel,
        in_specs=[WHOLE] * len(rows),
        out_specs=WHOLE,
        out_shape=out(rows[0].shape, f32),
        compiler_params=params(4),
        name="fold",
    )(*map(near, rows))


def slope_kernel(part, peers, tile, idx_ref, *refs):
    if peers:
        tops_ref = refs[peers]
        ez_ref, et_ref, ht_ref = refs[peers + 1:peers + 4]
        slope_ref, msg_ref, coef_ref, loss_ref = refs[peers + 4:]

        got = [r[...] for r in refs[:peers]]
        while len(got) > 1:
            got = [fold_rows(got[j], got[j + 1]) for j in range(0, len(got), 2)]
        s = got[0]
        t_inv = 1.0 / s[1:2]
        lse_t = s[0:1] + jnp.log(s[1:2])
        lse_z = s[3:4] + jnp.log(s[4:5])
        n = s.shape[1]
        per_token = s[2:3] * t_inv - lse_t + (1.0 + ce_weight) * lse_z - ce_weight * s[5:6]
        plane = jnp.sum(per_token[:, :n // 2], axis=1, keepdims=True) + jnp.sum(
            per_token[:, n // 2:], axis=1, keepdims=True
        )
        loss_ref[...] = jnp.broadcast_to(plane, loss_ref.shape)
        z_inv = (1.0 + ce_weight) / s[4:5]
        tops = tops_ref[...]
        rows = [jnp.exp(tops[0:1] - s[0:1]) * t_inv]
        rows += [jnp.exp(tops[p + 1:p + 2] - s[3:4]) * z_inv for p in range(PARTS)]
        rows += [tops[PARTS + 1:PARTS + 2]]
        rows += [jnp.zeros((128 - len(rows), n), f32)]
        coef_ref[...] = jnp.concatenate(rows).T

    else:
        coef_ref, ez_ref, et_ref, ht_ref, slope_ref, msg_ref = refs
    b = coef_ref[:, 0:1]
    a = coef_ref[:, part + 1:part + 2]
    id_col = coef_ref[:, PARTS + 1:PARTS + 2].astype(jnp.int32)
    deep, piece = msg_ref.shape
    rows = pl.ds(pl.multiple_of(idx_ref[0] * deep, deep), deep)
    for first in range(0, piece, tile):
        at = slice(first, first + tile)
        e_t = et_ref[:, part * piece + first:part * piece + first + tile]
        value = ez_ref[:, at].astype(f32) * a - e_t.astype(f32) * b
        column = lax.broadcasted_iota(jnp.int32, value.shape, 1) + (part * piece + first)
        value = jnp.where(column == id_col, value - ce_weight, value)
        slope = value.astype(bf16)
        slope_ref[:, at] = slope
        msg_ref[:, at] = dot(ht_ref[rows, :], slope).astype(bf16)


def slope_call(part, index, head_args, e_z, e_t, hid_t, deep, tile):
    n, piece = e_z.shape
    peers = len(head_args) - 1
    out_specs = [WHOLE, WHOLE]
    out_shape = [out((n, piece), bf16), out((deep, piece), bf16)]
    if peers:
        out_specs += [WHOLE, WHOLE]
        out_shape += [out((n, 128), f32), out((8, 128), f32)]
    args = [*head_args, e_z, e_t, hid_t]
    return pl.pallas_call(
        functools.partial(slope_kernel, part, peers, tile),
        grid_spec=pltpu.PrefetchScalarGridSpec(
            num_scalar_prefetch=1,
            grid=(1,),
            in_specs=[WHOLE] * len(args),
            out_specs=out_specs,
        ),
        out_shape=out_shape,
        compiler_params=params(16),
        cost_estimate=cost(2 * n * deep * piece, 6 * n * piece),
        name="slope",
    )(index, *map(near, args))


def finish_kernel(count, core_ref, *refs):
    out_ref = refs[-1]
    for k in range(2):

        @pl.when(pl.program_id(0) == k)
        def _(k=k):
            terms = refs[k * count:(k + 1) * count]
            out_ref[...] = sum(r[...].astype(f32) for r in terms)


def finish_call(part, core, earlier, mine, other):
    rows, piece = mine[0].shape
    count = len(mine)
    args = [near(x) for x in mine + other]
    in_specs = [WHOLE] * len(args)
    aliases = {}
    if earlier is not None:
        aliases = {1 + len(args): 0}
        args.append(earlier)
        in_specs.append(pl.BlockSpec(memory_space=pl.ANY))
    return pl.pallas_call(
        functools.partial(finish_kernel, count),
        grid_spec=pltpu.PrefetchScalarGridSpec(
            num_scalar_prefetch=1,
            grid=(2,),
            in_specs=in_specs,
            out_specs=pl.BlockSpec(
                (rows, piece), lambda i, s: (0, jnp.where(i == 0, s[0], 1 - s[0]) * PARTS + part)
            ),
        ),
        out_shape=jax.ShapeDtypeStruct((rows, 2 * PARTS * piece), f32),
        input_output_aliases=aliases,
        compiler_params=params(8),
        cost_estimate=cost(2 * rows * piece, 12 * rows * piece),
        name="finish",
    )(core, *args)


def loss_kernel(scale, z_ref, *refs):
    planes, out_ref = [r[...] for r in refs[:-1]], refs[-1]
    nz = len(planes)
    total = jnp.zeros(out_ref.shape, f32)
    for chip in range(nz):
        k = lax.rem(z_ref[0] - chip + nz, nz)
        term = planes[0]
        for j in range(1, nz):
            term = jnp.where(k == j, planes[j], term)
        total = total + term
    out_ref[...] = total * scale


def loss_call(z, planes, scale):
    return pl.pallas_call(
        functools.partial(loss_kernel, scale),
        grid_spec=pltpu.PrefetchScalarGridSpec(
            num_scalar_prefetch=1,
            grid=(1,),
            in_specs=[WHOLE] * len(planes),
            out_specs=WHOLE,
        ),
        out_shape=jax.ShapeDtypeStruct(planes[0].shape, f32),
        compiler_params=params(4),
        name="loss_sum",
    )(z, *planes)


def body(n_tok, n_voc, hidden, head, logits, ids):
    nz = n_tok // 2
    rows, dh = hidden.shape
    own_rows, share = head.shape
    half = share // 2
    piece = half // PARTS
    deep = 2 * own_rows
    tile = min(256, rows)
    wide = min(256, piece)
    me = lax.axis_index("tok")
    core = lax.rem(me, 2)
    z = lax.div(me, 2)
    voc = lax.axis_index("voc")
    width = dh // n_voc

    def here(kind, s):
        return z + jnp.where((lax.rem(z, 2) == 0) == (kind == "even"), s, -s)

    def inside(block):
        return jnp.logical_and(block >= 0, block < nz)

    def single(s):
        return not set(holders("even", nz, s)) & set(holders("odd", nz, s))

    def scalar(x):
        return jnp.reshape(x, (1,)).astype(jnp.int32)

    even = core == 0
    first_chip = z == 0
    row_of = {("own", 0): z}
    for s in range(1, nz):
        even_block, odd_block = here("even", s), here("odd", s)
        row_of["even", s] = jnp.clip(even_block, 0, nz - 1)
        row_of["odd", s] = jnp.clip(odd_block, 0, nz - 1)
        if single(s):
            either = jnp.where(inside(even_block), even_block, odd_block)
            row_of["even", s] = row_of["odd", s] = jnp.clip(either, 0, nz - 1)
    ahead = {
        "core": scalar(core),
        "z": scalar(z),
        "last": scalar(jnp.where(z == 0, nz - 1, 0)),
        "first": scalar(row_of["even", nz - 1]),
    }
    row_of = {k: v * deep for k, v in row_of.items()}
    col_of = [(voc ^ v) * width for v in range(n_voc)]
    vocab_start = voc * share + core * half
    (even, first_chip, ahead, row_of, col_of, vocab_start), head, hidden, logits, ids = (
        lax.optimization_barrier(
            ((even, first_chip, ahead, row_of, col_of, vocab_start), head, hidden, logits, ids)
        )
    )

    def swap(x):
        return lax.ppermute(x, "tok", [(i, i ^ 1) for i in range(n_tok)])

    def hop(x, pairs):
        return lax.ppermute(x, "tok", [(2 * a + k, 2 * b + k) for a, b in pairs for k in range(2)])

    def cross_hop(x, pairs):
        return lax.ppermute(
            x, "tok", [(2 * a + k, 2 * b + 1 - k) for a, b in pairs for k in range(2)]
        )

    def plane_swap(x, v):
        return lax.ppermute(x, "voc", [(w, w ^ v) for w in range(n_voc)])

    def cut(x, row, col, shape):
        row, col = (jnp.asarray(i, jnp.int32) for i in (row, col))
        return lax.dynamic_slice(x, (row, col), shape, allow_negative_indices=False)

    def mine(x, other=False):
        left, right = x[:, :half], x[:, half:]
        return jnp.where(even, right, left) if other else jnp.where(even, left, right)

    keep, send = mine(head), mine(head, True)
    blocks = []
    for p in range(PARTS):
        part = slice(p * piece, (p + 1) * piece)
        other = swap(send[:, part])
        blocks.append(
            jnp.where(
                even,
                jnp.concatenate([keep[:, part], other]),
                jnp.concatenate([other, keep[:, part]]),
            )
        )

    came = [{("own", 0): b, ("even", 0): b, ("odd", 0): b} for b in blocks]
    other_kind = {"even": "odd", "odd": "even"}
    for s in range(1, nz):
        for p in range(PARTS):
            for kind in ("even", "odd"):
                pairs = [(edge(kind, a), a) for a in holders(kind, nz, s)]
                if pairs:
                    came[p][kind, s] = hop(came[p][other_kind[kind], s - 1], pairs)

    hid = jnp.concatenate([hidden, swap(hidden)])
    hid_t = turn_call(hid, tile)
    tgt = mine(logits, True)
    tgt = swap(tgt)
    local = jnp.concatenate([ids, swap(ids)]) - vocab_start
    e_t, t_stat = target_call(ahead["core"], logits, tgt, local[:, None], tile)

    stats, e_z = [], []
    order = arrivals(nz)
    whole = [[came[p][k] for k in order] for p in range(PARTS)]
    early = [k for k in order if k[1] < nz - 1]
    for p in range(PARTS):
        acc = early_call(nz, ahead["z"], whole[p][:len(early)], hid, tile)
        w = whole[p][len(early):]
        w = w[0] if len(w) == 1 else jnp.where(first_chip, w[0], w[1])
        outs = last_call(p, ahead["last"], w, acc, hid, e_t, t_stat, stats, tile)
        e_z.append(outs[0])
        if p < PARTS - 1:
            stats.append(outs[1])
    mine_rows, turned, tops = outs[1:]

    x = fold_call([mine_rows, swap(turned)])
    bits = n_voc.bit_length() - 1
    done = 0
    while True:
        few = min(2, bits - done)
        peers = range((1 << few) - 1, 0, -1)
        got = {v: plane_swap(x, v << done) for v in peers}
        got = [x] + [got[v] for v in sorted(got)]
        done += few
        if done >= bits:
            break
        x = fold_call(got)

    msgs, slope = [], []
    for p in range(PARTS):
        head_args = got + [tops] if p == 0 else [coef]
        outs = slope_call(
            p, ahead["first"], head_args, e_z[p], e_t, hid_t, deep, wide
        )
        slope.append(outs[0])
        msgs.append(outs[1])
        if p == 0:
            coef, plane = outs[2:]

    def grad_rows(way, s, p):
        return dot(cut(hid_t, row_of[way, s], 0, (deep, 2 * rows)), slope[p])

    def add(x, *terms):
        for t in terms:
            if t is not None:
                x = x + t.astype(f32)
        return x

    got = [{} for _ in range(PARTS)]
    for s in range(nz - 1, 0, -1):
        for p in range(PARTS):
            for kind in ("even", "odd"):
                pairs = [(a, edge(kind, a)) for a in holders(kind, nz, s)]
                if not pairs:
                    continue
                back = {k: got[p].get((k, s + 1)) for k in other_kind}
                if s == nz - 1 and kind == "even":
                    msg = msgs[p]
                elif not single(s):
                    msg = add(grad_rows(kind, s, p), back[other_kind[kind]]).astype(bf16)
                elif kind == "even" or s == nz - 1:
                    msg = add(grad_rows(kind, s, p), *back.values()).astype(bf16)
                if s == 1 and kind == "even" and p == PARTS - 1:
                    low, high = msg[:own_rows], msg[own_rows:]
                    straight = hop(jnp.where(even, low, high), pairs)
                    across = cross_hop(jnp.where(even, high, low), pairs)
                    continue
                got[p][kind, s] = hop(msg, pairs)
    grad_head = None
    for p in range(PARTS):
        full = add(grad_rows("own", 0, p), got[p].get(("even", 1)), got[p].get(("odd", 1)))
        low, high = full[:own_rows], full[own_rows:]
        mine_terms = [jnp.where(even, low, high)]
        other_terms = [swap(jnp.where(even, high, low).astype(bf16))]
        if p == PARTS - 1:
            mine_terms.append(straight)
            other_terms.append(across)
        grad_head = finish_call(p, ahead["core"], grad_head, mine_terms, other_terms)

    late, plane, _ = lax.optimization_barrier((slope, plane, msgs[-1]))
    planes = [hop(plane, [(a, (a + k) % nz) for a in range(nz)]) for k in range(1, nz)]
    loss = loss_call(ahead["z"], [plane] + planes, 1.0 / (rows * n_tok))[0, 0]

    part = hidden_call(nz, ahead["z"], late, whole, dh, tile)
    part = part[:rows].astype(f32) + swap(part[rows:]).astype(f32)

    def wide_slice(v):
        return cut(part, 0, col_of[v], (rows, width))

    grad_hidden = wide_slice(0)
    for v in range(1, n_voc):
        came = plane_swap(wide_slice(v).astype(bf16), v)
        grad_hidden = grad_hidden + came.astype(f32)
    return loss, grad_hidden, grad_head


def solution(mesh):
    placed = (P("tok", None), P("tok", "voc"), P("tok", "voc"), P("tok"))
    n_tok, n_voc = mesh.shape["tok"], mesh.shape["voc"]
    return jax.shard_map(
        functools.partial(body, n_tok, n_voc),
        mesh=mesh,
        in_specs=placed,
        out_specs=(P(), P("tok", "voc"), P("tok", "voc")),
        check_vma=False,
    )
```

```python
import functools
import jax
import jax.numpy as jnp
from jax import lax
from jax.experimental import pallas as pl
from jax.experimental.pallas import tpu as pltpu
from jax.sharding import PartitionSpec as P


ce_weight = 0.5
PARTS = 2
f32, bf16 = jnp.float32, jnp.bfloat16


def dot(a, b):
    return lax.dot_general(a, b, (((1,), (0,)), ((), ())), preferred_element_type=f32)


def dot_nt(a, b):
    return lax.dot_general(a, b, (((1,), (1,)), ((), ())), preferred_element_type=f32)


def lanes(columns, like, first=0):
    lane = lax.broadcasted_iota(jnp.int32, like, 1)
    out = jnp.zeros(like, f32)
    for k, c in enumerate(columns):
        out = jnp.where(lane == first + k, c, out)
    return out


def block_of(kind, z, s):
    ahead = (z % 2 == 0) == (kind == "even")
    return z + s if ahead else z - s


def edge(kind, z):
    return z ^ 1 if kind == "even" else ((z + 1) ^ 1) - 1


def holders(kind, nz, s):
    return [z for z in range(nz) if 0 <= block_of(kind, z, s) < nz]


def arrivals(nz):
    return [("own", 0)] + [
        (kind, s) for s in range(1, nz) for kind in ("even", "odd") if holders(kind, nz, s)
    ]


def cost(flops, size, trans=0):
    return pl.CostEstimate(flops=flops, bytes_accessed=size, transcendentals=trans)


WHOLE = pl.BlockSpec(memory_space=pltpu.VMEM)


def near(x):
    return pltpu.with_memory_space_constraint(x, pltpu.VMEM)


def out(shape, dtype):
    return pltpu.VMEM(shape, dtype)


def params(size):
    return pltpu.CompilerParams(vmem_limit_bytes=size << 20)


def target_kernel(own_tiles, core_ref, mine_ref, came_ref, id_ref, e_ref, stat_ref, row_ref, turn_ref):
    step = pl.program_id(0)
    steps = pl.num_programs(0)
    t = jnp.where(step < own_tiles, mine_ref[...], came_ref[...]).astype(f32)
    at = pl.ds(pl.multiple_of(step * t.shape[0], t.shape[0]), t.shape[0])
    top = jnp.max(t, axis=1, keepdims=True)
    e = jnp.exp(t - top)
    e_ref[at, :] = e.astype(bf16)
    total = jnp.sum(e, axis=1, keepdims=True)
    first = jnp.sum(e * t, axis=1, keepdims=True)
    ids = id_ref[...].astype(f32)
    size = t.shape[0]
    stat = lanes([top, total, first, ids], (size, 128))
    stat_ref[at, :] = stat
    row = lax.broadcasted_iota(jnp.int32, (8, size), 0)
    rows = jnp.where(row < 3, stat.T[:8], 0.0)
    row_ref[:, at] = rows
    turned = lax.rem(step + steps // 2, steps) * size
    turn_ref[:, pl.ds(pl.multiple_of(turned, size), size)] = rows


def target_call(core, logits, came, ids, tile):
    rows, half = came.shape
    n, own_tiles = 2 * rows, rows // tile
    return pl.pallas_call(
        functools.partial(target_kernel, own_tiles),
        grid_spec=pltpu.PrefetchScalarGridSpec(
            num_scalar_prefetch=1,
            grid=(n // tile,),
            in_specs=[
                pl.BlockSpec((tile, half), lambda i, s: (jnp.minimum(i, own_tiles - 1), s[0])),
                pl.BlockSpec((tile, half), lambda i, s: (jnp.maximum(i - own_tiles, 0), 0)),
                pl.BlockSpec((tile, 1), lambda i, s: (i, 0)),
            ],
            out_specs=[WHOLE] * 4,
        ),
        out_shape=[
            out((n, half), bf16),
            out((n, 128), f32),
            out((8, n), f32),
            out((8, n), f32),
        ],
        compiler_params=params(16),
        cost_estimate=cost(8 * n * half, 4 * n * half, n * half),
        name="target_exps",
    )(core, logits, came, ids)


def turn_kernel(tile, x_ref, out_ref):
    for k in range(x_ref.shape[0] // tile):
        at = slice(k * tile, (k + 1) * tile)
        out_ref[:, at] = x_ref[at, :].T


def turn_call(x, tile):
    n, dh = x.shape
    return pl.pallas_call(
        functools.partial(turn_kernel, tile),
        in_specs=[WHOLE],
        out_specs=WHOLE,
        out_shape=out((dh, n), bf16),
        compiler_params=params(8),
        cost_estimate=cost(0, 4 * n * dh),
        name="turn",
    )(near(x))


def assemble(z, nz, count, refs, whole_ref, sem):
    deep = refs[0].shape[0]
    given = arrivals(nz)[:count]

    def place(block):
        return pl.ds(pl.multiple_of(block * deep, deep), deep)

    def each(act):
        for k, (kind, s) in enumerate(given):
            if kind == "own":
                act(k, z)
                continue
            sign = jnp.where((lax.rem(z, 2) == 0) == (kind == "even"), 1, -1)
            block = z + sign * s

            @pl.when(jnp.logical_and(block >= 0, block < nz))
            def _(k=k, block=block):
                act(k, block)

    def copy(k, block):
        return pltpu.make_async_copy(refs[k], whole_ref.at[place(block), :], sem.at[k])

    each(lambda k, block: copy(k, block).start())
    if count < len(arrivals(nz)):

        @pl.when(jnp.logical_or(z == 0, z == nz - 1))
        def _():
            hole = jnp.where(z == 0, nz - 1, 0)
            whole_ref[place(hole), :] = jnp.zeros((deep, whole_ref.shape[1]), bf16)

    return lambda: each(lambda k, block: copy(k, block).wait())


def early_kernel(nz, count, z_ref, *refs):
    w_refs = refs[:count]
    h_ref, acc_ref, whole_ref, sem = refs[count:]

    @pl.when(pl.program_id(0) == 0)
    def _():
        assemble(z_ref[0], nz, count, w_refs, whole_ref, sem)()

    tile = h_ref.shape[0] // pl.num_programs(0)
    at = pl.ds(pl.multiple_of(pl.program_id(0) * tile, tile), tile)
    acc_ref[at, :] = dot(h_ref[at, :], whole_ref[...])


def early_call(nz, z, blocks, hid, tile):
    n, dh = hid.shape
    piece = blocks[0].shape[1]
    return pl.pallas_call(
        functools.partial(early_kernel, nz, len(blocks)),
        grid_spec=pltpu.PrefetchScalarGridSpec(
            num_scalar_prefetch=1,
            grid=(n // tile,),
            in_specs=[pl.BlockSpec(memory_space=pl.ANY)] * len(blocks) + [WHOLE],
            out_specs=WHOLE,
            scratch_shapes=[
                pltpu.VMEM((dh, piece), bf16),
                pltpu.SemaphoreType.DMA((len(blocks),)),
            ],
        ),
        out_shape=out((n, piece), f32),
        compiler_params=params(10),
        cost_estimate=cost(2 * n * dh * piece, 6 * n * piece),
        name="early_draft",
    )(z, *blocks, near(hid))


def last_kernel(part, earlier, tile, at_ref, *refs):
    w_ref, acc_ref, h_ref, e_ref = refs[:4]
    stat_refs = refs[4:4 + earlier]
    outs = refs[4 + earlier:]
    n, piece = acc_ref.shape
    deep = w_ref.shape[0]
    block = pl.ds(pl.multiple_of(at_ref[0] * deep, deep), deep)
    like = (tile, 128)
    for k in range(n // tile):
        at = slice(k * tile, (k + 1) * tile)
        z = acc_ref[at, :] + dot(h_ref[at, block], w_ref[...])
        top = jnp.max(z, axis=1, keepdims=True)
        e = jnp.exp(z - top)
        outs[0][at, :] = e.astype(bf16)
        total = jnp.sum(e, axis=1, keepdims=True)
        weight = e_ref[at, part * piece:(part + 1) * piece].astype(f32)
        cross = jnp.sum(weight * z, axis=1, keepdims=True)
        stat = lanes([top, total, cross], like, 4 * part)
        if part < PARTS - 1:
            outs[1][at, :] = stat
            continue
        send_ref, turn_ref, tops_ref = outs[1:]
        for r in stat_refs:
            stat = stat + r[at, :]
        row = stat.T
        row = [row[k:k + 1] for k in range(4 * PARTS)]
        tops = row[::4]
        all_top = functools.reduce(jnp.maximum, tops)
        total = sum(row[1 + 4 * p] * jnp.exp(tops[p] - all_top) for p in range(PARTS))
        blank = jnp.zeros((1, tile), f32)
        rows = [blank] * 3 + [all_top, total, sum(row[2::4]), blank, blank]
        rows = jnp.concatenate(rows)
        send_ref[:, at] = rows
        turned = (k * tile + n // 2) % n
        turn_ref[:, turned:turned + tile] = rows
        tops_ref[:, at] = jnp.concatenate(tops + [blank] * (8 - len(tops)))


def last_call(part, at, w, acc, hid, weight, stats, tile):
    n, piece = acc.shape
    out_shape = [out((n, piece), bf16)]
    if part < PARTS - 1:
        stats = []
        out_shape += [out((n, 128), f32)]
    else:
        out_shape += [out((8, n), f32)] * 3
    return pl.pallas_call(
        functools.partial(last_kernel, part, len(stats), tile),
        grid_spec=pltpu.PrefetchScalarGridSpec(
            num_scalar_prefetch=1,
            grid=(1,),
            in_specs=[WHOLE] * (4 + len(stats)),
            out_specs=[WHOLE] * len(out_shape),
        ),
        out_shape=out_shape,
        compiler_params=params(10),
        cost_estimate=cost(2 * n * w.shape[0] * piece, 8 * n * piece, n * piece),
        name="last_draft",
    )(at, near(w), near(acc), near(hid), near(weight), *map(near, stats))


def hidden_kernel(nz, count, z_ref, *refs):
    slope_refs, w_refs = refs[:PARTS], refs[PARTS:PARTS + PARTS * count]
    out_ref, whole_ref, sem = refs[PARTS + PARTS * count:]

    @pl.when(pl.program_id(0) == 0)
    def _():
        waits = [
            assemble(
                z_ref[0], nz, count, w_refs[p * count:(p + 1) * count], whole_ref.at[p], sem.at[p]
            )
            for p in range(PARTS)
        ]
        for wait in waits:
            wait()

    tile = out_ref.shape[0]
    at = pl.ds(pl.multiple_of(pl.program_id(0) * tile, tile), tile)
    acc = dot_nt(slope_refs[0][at, :], whole_ref[0])
    for p in range(1, PARTS):
        acc = acc + dot_nt(slope_refs[p][at, :], whole_ref[p])
    out_ref[...] = acc.astype(bf16)


def hidden_call(nz, z, slope, blocks, dh, tile):
    n, piece = slope[0].shape
    count = len(blocks[0])
    row = lambda i, s: (i, 0)
    return pl.pallas_call(
        functools.partial(hidden_kernel, nz, count),
        grid_spec=pltpu.PrefetchScalarGridSpec(
            num_scalar_prefetch=1,
            grid=(n // tile,),
            in_specs=[WHOLE] * PARTS
            + [pl.BlockSpec(memory_space=pl.ANY)] * (PARTS * count),
            out_specs=pl.BlockSpec((tile, dh), row),
            scratch_shapes=[
                pltpu.VMEM((PARTS, dh, piece), bf16),
                pltpu.SemaphoreType.DMA((PARTS, count)),
            ],
        ),
        out_shape=jax.ShapeDtypeStruct((n, dh), bf16),
        compiler_params=params(16),
        cost_estimate=cost(2 * n * dh * piece * PARTS, 8 * n * piece),
        name="hidden_grad",
    )(z, *map(near, slope), *[b for bs in blocks for b in bs])


def fold_rows(a, b):
    t_top = jnp.maximum(a[0:1], b[0:1])
    fa, fb = jnp.exp(a[0:1] - t_top), jnp.exp(b[0:1] - t_top)
    z_top = jnp.maximum(a[3:4], b[3:4])
    ga, gb = jnp.exp(a[3:4] - z_top), jnp.exp(b[3:4] - z_top)
    rows = [
        t_top,
        a[1:2] * fa + b[1:2] * fb,
        a[2:3] * fa + b[2:3] * fb,
        z_top,
        a[4:5] * ga + b[4:5] * gb,
        a[5:6] + b[5:6],
    ]
    return jnp.concatenate(rows + [a[6:8]])


def fold_kernel(*refs):
    got = [r[...] for r in refs[:-1]]
    while len(got) > 1:
        got = [fold_rows(got[j], got[j + 1]) for j in range(0, len(got), 2)]
    refs[-1][...] = got[0]


def fold_call(rows):
    return pl.pallas_call(
        fold_kernel,
        in_specs=[WHOLE] * len(rows),
        out_specs=WHOLE,
        out_shape=out(rows[0].shape, f32),
        compiler_params=params(4),
        name="fold",
    )(*map(near, rows))


def weight_kernel(peers, tile, *refs):
    local_ref, e_ref, stat_ref, w_ref, row_ref = refs[peers:]
    got = [r[...] for r in refs[:peers]]
    while len(got) > 1:
        got = [fold_rows(got[j], got[j + 1]) for j in range(0, len(got), 2)]
    s = got[0]
    n = s.shape[1]
    inv = 1.0 / s[1:2]
    row = s[2:3] * inv - s[0:1] - jnp.log(s[1:2])
    row_ref[...] = jnp.broadcast_to(row, row_ref.shape)
    gain = jnp.exp(local_ref[0:1, :] - s[0:1]) * inv
    gain = jnp.concatenate([gain, jnp.zeros((127, n), f32)]).T[:, 0:1]
    id_col = stat_ref[:, 3:4].astype(jnp.int32)
    for first in range(0, e_ref.shape[1], tile):
        at = slice(first, first + tile)
        value = e_ref[:, at].astype(f32) * gain
        column = lax.broadcasted_iota(jnp.int32, value.shape, 1) + first
        w_ref[:, at] = jnp.where(column == id_col, value + ce_weight, value).astype(bf16)


def weight_call(got, local, e_t, t_stat, tile):
    n, half = e_t.shape
    args = [*got, local, e_t, t_stat]
    return pl.pallas_call(
        functools.partial(weight_kernel, len(got), tile),
        in_specs=[WHOLE] * len(args),
        out_specs=[WHOLE, WHOLE],
        out_shape=[out((n, half), bf16), out((8, n), f32)],
        compiler_params=params(16),
        cost_estimate=cost(4 * n * half, 4 * n * half),
        name="weights",
    )(*map(near, args))


def slope_kernel(part, peers, tile, idx_ref, *refs):
    if peers:
        tops_ref, t_ref = refs[peers:peers + 2]
        ez_ref, w_ref, ht_ref = refs[peers + 2:peers + 5]
        slope_ref, msg_ref, coef_ref, loss_ref = refs[peers + 5:]
        got = [r[...] for r in refs[:peers]]
        while len(got) > 1:
            got = [fold_rows(got[j], got[j + 1]) for j in range(0, len(got), 2)]
        s = got[0]
        n = s.shape[1]
        lse_z = s[3:4] + jnp.log(s[4:5])
        per_token = t_ref[0:1, :] - s[5:6] + (1.0 + ce_weight) * lse_z
        plane = jnp.sum(per_token[:, :n // 2], axis=1, keepdims=True) + jnp.sum(
            per_token[:, n // 2:], axis=1, keepdims=True
        )
        loss_ref[...] = jnp.broadcast_to(plane, loss_ref.shape)
        z_inv = (1.0 + ce_weight) / s[4:5]
        tops = tops_ref[...]
        rows = [jnp.exp(tops[p:p + 1] - s[3:4]) * z_inv for p in range(PARTS)]
        rows += [jnp.zeros((128 - len(rows), n), f32)]
        coef_ref[...] = jnp.concatenate(rows).T
    else:
        coef_ref, ez_ref, w_ref, ht_ref, slope_ref, msg_ref = refs
    a = coef_ref[:, part:part + 1]
    deep, piece = msg_ref.shape
    rows = pl.ds(pl.multiple_of(idx_ref[0] * deep, deep), deep)
    for first in range(0, piece, tile):
        at = slice(first, first + tile)
        weight = w_ref[:, part * piece + first:part * piece + first + tile]
        slope = (ez_ref[:, at].astype(f32) * a - weight.astype(f32)).astype(bf16)
        slope_ref[:, at] = slope
        msg_ref[:, at] = dot(ht_ref[rows, :], slope).astype(bf16)


def slope_call(part, index, head_args, e_z, weight, hid_t, deep, tile):
    n, piece = e_z.shape
    peers = max(0, len(head_args) - 2)
    out_specs = [WHOLE, WHOLE]
    out_shape = [out((n, piece), bf16), out((deep, piece), bf16)]
    if peers:
        out_specs += [WHOLE, WHOLE]
        out_shape += [out((n, 128), f32), out((8, 128), f32)]
    args = [*head_args, e_z, weight, hid_t]
    return pl.pallas_call(
        functools.partial(slope_kernel, part, peers, tile),
        grid_spec=pltpu.PrefetchScalarGridSpec(
            num_scalar_prefetch=1,
            grid=(1,),
            in_specs=[WHOLE] * len(args),
            out_specs=out_specs,
        ),
        out_shape=out_shape,
        compiler_params=params(16),
        cost_estimate=cost(2 * n * deep * piece, 6 * n * piece),
        name="slope",
    )(index, *map(near, args))


def finish_kernel(count, core_ref, *refs):
    out_ref = refs[-1]
    for k in range(2):

        @pl.when(pl.program_id(0) == k)
        def _(k=k):
            terms = refs[k * count:(k + 1) * count]
            out_ref[...] = sum(r[...].astype(f32) for r in terms)


def finish_call(part, core, earlier, mine, other):
    rows, piece = mine[0].shape
    count = len(mine)
    args = [near(x) for x in mine + other]
    in_specs = [WHOLE] * len(args)
    aliases = {}
    if earlier is not None:
        aliases = {1 + len(args): 0}
        args.append(earlier)
        in_specs.append(pl.BlockSpec(memory_space=pl.ANY))
    return pl.pallas_call(
        functools.partial(finish_kernel, count),
        grid_spec=pltpu.PrefetchScalarGridSpec(
            num_scalar_prefetch=1,
            grid=(2,),
            in_specs=in_specs,
            out_specs=pl.BlockSpec(
                (rows, piece), lambda i, s: (0, jnp.where(i == 0, s[0], 1 - s[0]) * PARTS + part)
            ),
        ),
        out_shape=jax.ShapeDtypeStruct((rows, 2 * PARTS * piece), f32),
        input_output_aliases=aliases,
        compiler_params=params(8),
        cost_estimate=cost(2 * rows * piece, 12 * rows * piece),
        name="finish",
    )(core, *args)


def loss_kernel(scale, z_ref, *refs):
    planes, out_ref = [r[...] for r in refs[:-1]], refs[-1]
    nz = len(planes)
    total = jnp.zeros(out_ref.shape, f32)
    for chip in range(nz):
        k = lax.rem(z_ref[0] - chip + nz, nz)
        term = planes[0]
        for j in range(1, nz):
            term = jnp.where(k == j, planes[j], term)
        total = total + term
    out_ref[...] = total * scale


def loss_call(z, planes, scale):
    return pl.pallas_call(
        functools.partial(loss_kernel, scale),
        grid_spec=pltpu.PrefetchScalarGridSpec(
            num_scalar_prefetch=1,
            grid=(1,),
            in_specs=[WHOLE] * len(planes),
            out_specs=WHOLE,
        ),
        out_shape=jax.ShapeDtypeStruct(planes[0].shape, f32),
        compiler_params=params(4),
        name="loss_sum",
    )(z, *planes)


def body(n_tok, n_voc, hidden, head, logits, ids):
    nz = n_tok // 2
    rows, dh = hidden.shape
    own_rows, share = head.shape
    half = share // 2
    piece = half // PARTS
    deep = 2 * own_rows
    tile = min(256, rows)
    wide = min(256, piece)
    me = lax.axis_index("tok")
    core = lax.rem(me, 2)
    z = lax.div(me, 2)
    voc = lax.axis_index("voc")
    width = dh // n_voc

    def here(kind, s):
        return z + jnp.where((lax.rem(z, 2) == 0) == (kind == "even"), s, -s)

    def inside(block):
        return jnp.logical_and(block >= 0, block < nz)

    def single(s):
        return not set(holders("even", nz, s)) & set(holders("odd", nz, s))

    def scalar(x):
        return jnp.reshape(x, (1,)).astype(jnp.int32)

    even = core == 0
    first_chip = z == 0
    row_of = {("own", 0): z}
    for s in range(1, nz):
        even_block, odd_block = here("even", s), here("odd", s)
        row_of["even", s] = jnp.clip(even_block, 0, nz - 1)
        row_of["odd", s] = jnp.clip(odd_block, 0, nz - 1)
        if single(s):
            either = jnp.where(inside(even_block), even_block, odd_block)
            row_of["even", s] = row_of["odd", s] = jnp.clip(either, 0, nz - 1)
    ahead = {
        "core": scalar(core),
        "z": scalar(z),
        "last": scalar(jnp.where(z == 0, nz - 1, 0)),
        "first": scalar(row_of["even", nz - 1]),
    }
    row_of = {k: v * deep for k, v in row_of.items()}
    col_of = [(voc ^ v) * width for v in range(n_voc)]
    vocab_start = voc * share + core * half
    (even, first_chip, ahead, row_of, col_of, vocab_start), head, hidden, logits, ids = (
        lax.optimization_barrier(
            ((even, first_chip, ahead, row_of, col_of, vocab_start), head, hidden, logits, ids)
        )
    )

    def swap(x):
        return lax.ppermute(x, "tok", [(i, i ^ 1) for i in range(n_tok)])

    def hop(x, pairs):
        return lax.ppermute(x, "tok", [(2 * a + k, 2 * b + k) for a, b in pairs for k in range(2)])

    def cross_hop(x, pairs):
        return lax.ppermute(
            x, "tok", [(2 * a + k, 2 * b + 1 - k) for a, b in pairs for k in range(2)]
        )

    def plane_swap(x, v):
        return lax.ppermute(x, "voc", [(w, w ^ v) for w in range(n_voc)])

    def cut(x, row, col, shape):
        row, col = (jnp.asarray(i, jnp.int32) for i in (row, col))
        return lax.dynamic_slice(x, (row, col), shape, allow_negative_indices=False)

    def mine(x, other=False):
        left, right = x[:, :half], x[:, half:]
        return jnp.where(even, right, left) if other else jnp.where(even, left, right)

    keep, send = mine(head), mine(head, True)
    blocks = []
    for p in range(PARTS):
        part = slice(p * piece, (p + 1) * piece)
        other = swap(send[:, part])
        blocks.append(
            jnp.where(
                even,
                jnp.concatenate([keep[:, part], other]),
                jnp.concatenate([other, keep[:, part]]),
            )
        )

    came = [{("own", 0): b, ("even", 0): b, ("odd", 0): b} for b in blocks]
    other_kind = {"even": "odd", "odd": "even"}
    for s in range(1, nz):
        for p in range(PARTS):
            for kind in ("even", "odd"):
                pairs = [(edge(kind, a), a) for a in holders(kind, nz, s)]
                if pairs:
                    came[p][kind, s] = hop(came[p][other_kind[kind], s - 1], pairs)

    hid = jnp.concatenate([hidden, swap(hidden)])
    hid_t = turn_call(hid, tile)
    tgt = mine(logits, True)
    tgt = swap(tgt)
    local = jnp.concatenate([ids, swap(ids)]) - vocab_start
    e_t, t_stat, t_rows, t_turned = target_call(ahead["core"], logits, tgt, local[:, None], tile)

    def exchange(rows, turned):
        x = fold_call([rows, swap(turned)])
        bits = n_voc.bit_length() - 1
        done = 0
        while True:
            few = min(2, bits - done)
            peers = range((1 << few) - 1, 0, -1)
            got = {v: plane_swap(x, v << done) for v in peers}
            got = [x] + [got[v] for v in sorted(got)]
            done += few
            if done >= bits:
                return got
            x = fold_call(got)

    got = exchange(t_rows, t_turned)
    weight, t_row = weight_call(got, t_rows, e_t, t_stat, wide)

    stats, e_z = [], []
    order = arrivals(nz)
    whole = [[came[p][k] for k in order] for p in range(PARTS)]
    early = [k for k in order if k[1] < nz - 1]
    for p in range(PARTS):
        acc = early_call(nz, ahead["z"], whole[p][:len(early)], hid, tile)
        w = whole[p][len(early):]
        w = w[0] if len(w) == 1 else jnp.where(first_chip, w[0], w[1])
        outs = last_call(p, ahead["last"], w, acc, hid, weight, stats, tile)
        e_z.append(outs[0])
        if p < PARTS - 1:
            stats.append(outs[1])
    mine_rows, turned, tops = outs[1:]

    got = exchange(mine_rows, turned)

    msgs, slope = [], []
    for p in range(PARTS):
        head_args = got + [tops, t_row] if p == 0 else [coef]
        outs = slope_call(
            p, ahead["first"], head_args, e_z[p], weight, hid_t, deep, wide
        )
        slope.append(outs[0])
        msgs.append(outs[1])
        if p == 0:
            coef, plane = outs[2:]

    def grad_rows(way, s, p):
        return dot(cut(hid_t, row_of[way, s], 0, (deep, 2 * rows)), slope[p])

    def add(x, *terms):
        for t in terms:
            if t is not None:
                x = x + t.astype(f32)
        return x

    got = [{} for _ in range(PARTS)]
    for s in range(nz - 1, 0, -1):
        for p in range(PARTS):
            for kind in ("even", "odd"):
                pairs = [(a, edge(kind, a)) for a in holders(kind, nz, s)]
                if not pairs:
                    continue
                back = {k: got[p].get((k, s + 1)) for k in other_kind}
                if s == nz - 1 and kind == "even":
                    msg = msgs[p]
                elif not single(s):
                    msg = add(grad_rows(kind, s, p), back[other_kind[kind]]).astype(bf16)
                elif kind == "even" or s == nz - 1:
                    msg = add(grad_rows(kind, s, p), *back.values()).astype(bf16)
                if s == 1 and kind == "even" and p == PARTS - 1:
                    low, high = msg[:own_rows], msg[own_rows:]
                    straight = hop(jnp.where(even, low, high), pairs)
                    across = cross_hop(jnp.where(even, high, low), pairs)
                    continue
                got[p][kind, s] = hop(msg, pairs)
    grad_head = None
    for p in range(PARTS):
        full = add(grad_rows("own", 0, p), got[p].get(("even", 1)), got[p].get(("odd", 1)))
        low, high = full[:own_rows], full[own_rows:]
        mine_terms = [jnp.where(even, low, high)]
        other_terms = [swap(jnp.where(even, high, low).astype(bf16))]
        if p == PARTS - 1:
            mine_terms.append(straight)
            other_terms.append(across)
        grad_head = finish_call(p, ahead["core"], grad_head, mine_terms, other_terms)

    late, plane, _ = lax.optimization_barrier((slope, plane, msgs[-1]))
    planes = [hop(plane, [(a, (a + k) % nz) for a in range(nz)]) for k in range(1, nz)]
    loss = loss_call(ahead["z"], [plane] + planes, 1.0 / (rows * n_tok))[0, 0]

    part = hidden_call(nz, ahead["z"], late, whole, dh, tile)
    part = part[:rows].astype(f32) + swap(part[rows:]).astype(f32)

    def wide_slice(v):
        return cut(part, 0, col_of[v], (rows, width))

    grad_hidden = wide_slice(0)
    for v in range(1, n_voc):
        came = plane_swap(wide_slice(v).astype(bf16), v)
        grad_hidden = grad_hidden + came.astype(f32)
    return loss, grad_hidden, grad_head


def solution(mesh):
    placed = (P("tok", None), P("tok", "voc"), P("tok", "voc"), P("tok"))
    n_tok, n_voc = mesh.shape["tok"], mesh.shape["voc"]
    return jax.shard_map(
        functools.partial(body, n_tok, n_voc),
        mesh=mesh,
        in_specs=placed,
        out_specs=(P(), P("tok", "voc"), P("tok", "voc")),
        check_vma=False,
    )
```
